256 devices in a mesh: row: 32 (over x, y, core), col: 8 (over z).
Axes of the slice: x: 4, y: 4, z: 8, core: 2. Of those that a mesh axis runs over, the one named last changes fastest.
Arguments:
- features: bfloat16 [65536, 256], P(('row', 'col')), may hold values from -6 to 6
- weight: bfloat16 [256, 256], replicated, may hold values from -0.375 to 0.375
- tile_values: bfloat16 [24576, 128, 128], P(('row', 'col')), may hold values from -0.21582031 to 0.21582031
- tile_coords: int32 [24576, 2], P(('row', 'col')), may hold values from 0 to 63, as said below
- tile_count: int32 [256], P(('row', 'col')), may hold values from 1 to 96, as said below
- cotangent: bfloat16 [65536, 256], P(('row', 'col')), may hold values from -6 to 6
Outputs:
- hidden: bfloat16 [65536, 256], P(('row', 'col'))
- weight_grad: float32 [256, 256], P('row')
- feature_grad: float32 [65536, 256], P(('row', 'col'))
The draws below stay inside these ranges and needn't reach their ends.
Inputs may be any that keep to these rules, and one draw needn't show every extreme that they name: Device d = a 8 + b uses its first tile_count[d] slots; some device uses all 96. `tile_coords`: column 0 is a local row tile below 16, column 1 a local column tile below 64. A device's 96 slots name distinct (row tile, column tile) positions.
All inputs are finite; a program needn't handle non-finite values.
Results may differ from the reference program's by a relative error of at most 0.006.
Values may be sent and summed in bfloat16 or wider, within the bound.
A program may use at most 128 MiB of HBM per device.

```python
import jax
import jax.numpy as jnp
from jax import lax

F = 256
TILE = 128
ROWS_DEV = 256
TILE_DEV = 96
NODES = 65536
ROW_TILES = 16
COL_TILES = 64
N_ROW = 32
N_COL = 8


def draw_tile_count(key, part):
    devices_all = N_ROW * N_COL
    first_key, second_key = jax.random.split(jax.random.fold_in(key, 7))
    spread = jax.random.randint(first_key, (devices_all,), 0, TILE_DEV + 1)
    counts = TILE_DEV // 16 + spread * spread // TILE_DEV
    counts = jnp.clip(counts, 1, TILE_DEV)
    busiest = jax.random.randint(second_key, (), 0, devices_all)
    counts = jnp.where(jnp.arange(devices_all) == busiest, TILE_DEV, counts)
    return counts.astype(jnp.int32)


def draw_tile_coords(key, part):
    devices_all = N_ROW * N_COL
    positions = ROW_TILES * COL_TILES
    keys = jax.random.split(jax.random.fold_in(key, 11), devices_all)
    orders = jax.vmap(lambda one_key: jax.random.permutation(one_key, positions))(keys)
    repeats = (TILE_DEV + positions - 1) // positions
    chosen = jnp.tile(orders, (1, repeats))[:, :TILE_DEV]
    row_part = chosen // COL_TILES
    col_part = chosen % COL_TILES
    return jnp.stack([row_part, col_part], axis=-1).reshape(devices_all * TILE_DEV, 2).astype(jnp.int32)


def block_scale(rng, shape, cuts, smallest, high):
    factor_of = 1.0
    for axis_at, blocks in cuts:
        steps = jax.random.uniform(jax.random.fold_in(jax.random.fold_in(rng, 6), axis_at), (blocks,), jnp.float32, smallest / len(cuts), high / len(cuts))
        factor_of = factor_of * jnp.repeat(jnp.exp(steps), shape[axis_at] // blocks).reshape((-1,) + (1,) * (len(shape) - 1 - axis_at))
    return factor_of


def gaussian(stream_key, extent, deviation, reach, pieces=(), held_as=jnp.bfloat16):
    factor_of = block_scale(stream_key, extent, pieces, -0.22, 0.18) if pieces else 1.0
    array = jax.random.normal(stream_key, extent, jnp.float32) * deviation * factor_of
    return jnp.minimum(jnp.maximum(array, -reach), reach).astype(held_as)


def setup_inputs(seed: int = 0) -> dict:
    splits = jax.random.split(jax.random.key(seed), 7)
    features = gaussian(splits[0], (NODES, F), 1.0, 6.0, ((0, 256),))
    weight = gaussian(splits[1], (F, F), F ** -0.5, 0.375)
    tile_values = gaussian(splits[2], (NODES * TILE_DEV // ROWS_DEV, TILE, TILE), ((TILE * TILE_DEV // 16) ** -0.5), 0.21582031, ((0, 256),))
    tile_coords = draw_tile_coords(jax.random.fold_in(splits[6], 71), 0)
    tile_count = draw_tile_count(jax.random.fold_in(splits[6], 71), 0)
    cotangent = gaussian(splits[5], (NODES, F), 1.0, 6.0, ((0, 256),))
    return {"features": features, "weight": weight, "tile_values": tile_values, "tile_coords": tile_coords, "tile_count": tile_count, "cotangent": cotangent}


gelu_scale = 0.7978845608028654
gelu_cubic = 0.044715


def gelu_pair(values):
    inner = gelu_scale * (values + gelu_cubic * values * values * values)
    slope_tanh = jnp.tanh(inner)
    result = 0.5 * values * (1.0 + slope_tanh)
    slope = 0.5 * (1.0 + slope_tanh) + 0.5 * values * (1.0 - slope_tanh * slope_tanh) * gelu_scale * (1.0 + 3.0 * gelu_cubic * values * values)
    return result, slope


def reference(features, weight, tile_values, tile_coords, tile_count, cotangent):
    tile_grid = tile_values.reshape(N_ROW, N_COL, TILE_DEV, TILE, TILE)
    coord_grid = tile_coords.reshape(N_ROW, N_COL, TILE_DEV, 2)
    count_grid = tile_count.reshape(N_ROW, N_COL)
    feat_grid = features.reshape(N_ROW, N_COL, ROWS_DEV, F)
    slot_ids = jnp.arange(TILE_DEV, dtype=jnp.int32)

    def forward_block(row_at):
        def add_device(total, col_at):
            tiles = tile_grid[row_at, col_at].astype(jnp.float32)
            coords = coord_grid[row_at, col_at]
            live = slot_ids < count_grid[row_at, col_at]
            source = feat_grid[:, col_at].reshape(COL_TILES, TILE, F).astype(jnp.float32)
            picked = source[coords[:, 1]]
            products = jnp.einsum("kab,kbf->kaf", tiles, picked, precision=lax.Precision.HIGHEST)
            products = jnp.where(live[:, None, None], products, jnp.zeros_like(products))
            summed = jax.ops.segment_sum(products, coords[:, 0], num_segments=ROW_TILES)
            return total + summed, None

        total, unused = lax.scan(add_device, jnp.zeros((ROW_TILES, TILE, F), jnp.float32), jnp.arange(N_COL, dtype=jnp.int32))
        return total

    aggregated = lax.map(forward_block, jnp.arange(N_ROW, dtype=jnp.int32)).reshape(NODES, F)
    agg_rows = aggregated.astype(jnp.bfloat16)
    pre = jnp.dot(agg_rows, weight, preferred_element_type=jnp.float32)
    result, slope = gelu_pair(pre)
    hidden = result.astype(jnp.bfloat16)
    grad_pre = (cotangent.astype(jnp.float32) * slope).astype(jnp.bfloat16)
    weight_grad = jnp.dot(agg_rows.T, grad_pre, preferred_element_type=jnp.float32)
    grad_agg = jnp.dot(grad_pre, weight.T, preferred_element_type=jnp.float32).astype(jnp.bfloat16)
    grad_grid = grad_agg.reshape(N_ROW, ROW_TILES, TILE, F)

    def backward_set(col_at):
        def add_device(total, row_at):
            tiles = tile_grid[row_at, col_at].astype(jnp.float32)
            coords = coord_grid[row_at, col_at]
            live = slot_ids < count_grid[row_at, col_at]
            picked = grad_grid[row_at][coords[:, 0]].astype(jnp.float32)
            products = jnp.einsum("kba,kbf->kaf", tiles, picked, precision=lax.Precision.HIGHEST)
            products = jnp.where(live[:, None, None], products, jnp.zeros_like(products))
            summed = jax.ops.segment_sum(products, coords[:, 1], num_segments=COL_TILES)
            return total + summed, None

        total, unused = lax.scan(add_device, jnp.zeros((COL_TILES, TILE, F), jnp.float32), jnp.arange(N_ROW, dtype=jnp.int32))
        return total

    col_sets = lax.map(backward_set, jnp.arange(N_COL, dtype=jnp.int32))
    feature_grad = col_sets.reshape(N_COL, N_ROW, ROWS_DEV, F).transpose(1, 0, 2, 3).reshape(NODES, F)
    return hidden, weight_grad, feature_grad
```

```python
import functools

import jax
import jax.numpy as jnp
from jax import lax
from jax.experimental import pallas as pl
from jax.experimental.pallas import tpu as pltpu
from jax.sharding import PartitionSpec as P

gelu_scale = 0.7978845608028654
gelu_cubic = 0.044715

MESH = pl.DeviceIdType.MESH
BF16 = jnp.bfloat16
F32 = jnp.float32
T = 128
HALF = 64
SIDE = 4
RING = 8
SLOTS = 96
ROW_TILES = 16
COL_TILES = 64
UNROLL = 4

PREV_F, LAST_F, PREV_B, LAST_B, ROW_ID, COL_ID = range(6)

OFFS = (0, -1, 1, 2)


def gelu_pair(values):
    inner = gelu_scale * (values + gelu_cubic * values * values * values)
    slope_tanh = jnp.tanh(inner)
    result = 0.5 * values * (1.0 + slope_tanh)
    slope = 0.5 * (1.0 + slope_tanh) + 0.5 * values * (
        1.0 - slope_tanh * slope_tanh
    ) * gelu_scale * (1.0 + 3.0 * gelu_cubic * values * values)
    return (result, slope)


def scratch():
    tile2 = (2, T, T)
    dma = pltpu.SemaphoreType.DMA
    return {
        "tiles": pltpu.VMEM((SLOTS, T, T), BF16),
        "weight_v": pltpu.VMEM((256, 256), BF16),
        "cot_v": pltpu.VMEM((256, 256), BF16),
        "coords_v": pltpu.VMEM((SLOTS, 2), jnp.int32),
        "table_v": pltpu.VMEM((8, T), jnp.int32),
        "table": pltpu.SMEM((8, T), jnp.int32),
        "panel0": pltpu.VMEM((COL_TILES, T, T), BF16),
        "panel1": pltpu.VMEM((COL_TILES, T, T), BF16),
        "sums0": pltpu.VMEM((SLOTS + 1, T, T), F32),
        "sums1": pltpu.VMEM((SLOTS + 1, T, T), F32),
        "zs": pltpu.VMEM((2, 2, 4) + tile2, BF16),
        "zr": pltpu.VMEM((2, 2, 4) + tile2, BF16),
        "agg": pltpu.VMEM((256, 256), BF16),
        "hid_v": pltpu.VMEM((256, 256), BF16),
        "wg": pltpu.VMEM((32, 8, 256), F32),
        "wg_row": pltpu.VMEM((32, 8, 256), F32),
        "wg_part": pltpu.VMEM((8, 256), F32),
        "wg_col": pltpu.VMEM((8, 8, 256), F32),
        "wg_out": pltpu.VMEM((8, 256), F32),
        "ga0": pltpu.VMEM((ROW_TILES, T, T), BF16),
        "ga1": pltpu.VMEM((ROW_TILES, T, T), BF16),
        "ps": pltpu.VMEM((2, 2, 4, 4, T, T), BF16),
        "pr": pltpu.VMEM((2, 2, 4, 4, T, T), BF16),
        "s1": pltpu.VMEM((2, 2, 4, T, T), BF16),
        "r1": pltpu.VMEM((2, 2, 2, 4, HALF, T), BF16),
        "s2": pltpu.VMEM((2, 2, 2, 4, T, T), BF16),
        "r2": pltpu.VMEM((2, 2, 2, 4, T, T), BF16),
        "axis_sum": pltpu.VMEM((2, 2, 4, T, T), F32),
        "s3": pltpu.VMEM((2, 2, T, T), BF16),
        "r3": pltpu.VMEM((2, 2, 2, HALF, T), BF16),
        "s4": pltpu.VMEM((2, 2, 2, T, T), BF16),
        "r4": pltpu.VMEM((2, 2, 2, T, T), BF16),
        "fg_v": pltpu.VMEM((256, 256), F32),
        "local_sem": dma((12,)),
        "send_sem": dma((240,)),
        "a_sem": dma((2, 2, 20)),
        "ap_sem": dma((2, 2, 16)),
        "z_sem": dma((2, 2, 4)),
        "d_sem": dma((2, 2, 4)),
        "p_sem": dma((2, 2, 4)),
        "r1_sem": dma((2, 2, 2)),
        "r2_sem": dma((2, 2, 2)),
        "r3_sem": dma((2, 2, 2)),
        "r4_sem": dma((2, 2, 2)),
        "wr_send": dma((32,)),
        "wr_recv": dma((32,)),
        "wc_send": dma((8,)),
        "wc_recv": dma((8,)),
    }


class Layer:
    def __init__(self, count, features, weight, tile_values, coords, cotangent, hidden, weight_grad, feature_grad, refs):
        self.__dict__.update(refs)
        self.count = count
        self.features, self.weight, self.tile_values = features, weight, tile_values
        self.coords, self.cotangent = coords, cotangent
        self.hidden, self.weight_grad, self.feature_grad = hidden, weight_grad, feature_grad
        self.panel = (self.panel0, self.panel1)
        self.sums = (self.sums0, self.sums1)
        self.ga = (self.ga0, self.ga1)
        self.row = lax.axis_index("row")
        self.z = lax.axis_index("col")
        self.core = lax.rem(self.row, 2)
        self.at = (self.row // 8, lax.rem(self.row // 2, SIDE))
        self.sends = []

    def along(self, axis, step):
        return lax.rem(self.at[axis] + step % SIDE, SIDE)

    def row_of(self, x, y, core):
        return (x * SIDE + y) * 2 + core

    def neighbour(self, axis, step):
        spot = [self.at[0], self.at[1]]
        spot[axis] = self.along(axis, step)
        return (self.row_of(spot[0], spot[1], self.core), self.z)

    def partner(self):
        return (self.row_of(self.at[0], self.at[1], 1 - self.core), self.z)

    def ring(self, step):
        return lax.rem(self.z + step % RING, RING)

    def tile_at(self, piece, first, second, core):
        x, y = (first, second) if piece == 0 else (second, first)
        return self.row_of(x, y, core) * 2 + piece

    def near_tile(self, piece, step1, step2, core):
        first, second = piece, 1 - piece
        return self.tile_at(piece, self.along(first, step1), self.along(second, step2), core)

    def send(self, src, dst, sem, device):
        copy = pltpu.make_async_remote_copy(
            src_ref=src, dst_ref=dst, send_sem=self.send_sem.at[len(self.sends)],
            recv_sem=sem, device_id=device, device_id_type=MESH,
        )
        copy.start()
        self.sends.append(copy)

    def arrive(self, dst, sem):
        pltpu.make_async_remote_copy(
            src_ref=dst, dst_ref=dst, send_sem=self.send_sem.at[0],
            recv_sem=sem, device_id=self.partner(), device_id_type=MESH,
        ).wait_recv()

    def load(self):
        sem = self.local_sem
        half = [
            pltpu.make_async_copy(
                self.features.at[:, :, pl.ds(h * T, T)],
                self.panel[h].at[pl.ds(self.row * 2, 2)], sem.at[h])
            for h in range(2)
        ]
        coords = pltpu.make_async_copy(self.coords, self.coords_v, sem.at[2])
        tiles = pltpu.make_async_copy(self.tile_values, self.tiles, sem.at[3])
        weight = pltpu.make_async_copy(self.weight, self.weight_v, sem.at[4])
        cot = pltpu.make_async_copy(self.cotangent, self.cot_v, sem.at[5])
        for copy in (*half, coords, tiles, weight, cot):
            copy.start()
        self.own, self.coords_in, self.tiles_in, self.dense_in = half, coords, tiles, (weight, cot)

    def neighbours(self):
        return [
            self.partner(), self.neighbour(0, 1), self.neighbour(0, -1), self.neighbour(1, 1),
            self.neighbour(1, -1), (self.row, self.ring(1)), (self.row, self.ring(-1)),
        ]

    def greet(self):
        barrier = pltpu.get_barrier_semaphore()
        for device in self.neighbours():
            pl.semaphore_signal(barrier, inc=1, device_id=device, device_id_type=MESH)

    def met(self):
        pl.semaphore_wait(pltpu.get_barrier_semaphore(), 7)

    def index_table(self):
        self.coords_in.wait()
        slot = lax.broadcasted_iota(jnp.int32, (SLOTS, T), 0)
        lane = lax.broadcasted_iota(jnp.int32, (SLOTS, T), 1)
        live = slot < self.count[0]
        lines = [None] * 8
        for column, prev, last, ids in ((0, PREV_F, LAST_F, ROW_ID), (1, PREV_B, LAST_B, COL_ID)):
            down = jnp.broadcast_to(self.coords_v[:, column:column + 1], (SLOTS, T))
            across = jnp.sum(jnp.where(slot == lane, down, 0), axis=0, keepdims=True)
            earlier = live & (slot < lane) & (down == across)
            lines[prev] = jnp.max(jnp.where(earlier, slot + 1, 0), axis=0, keepdims=True)
            lines[last] = jnp.max(jnp.where(live & (down == lane), slot + 1, 0), axis=0, keepdims=True)
            lines[ids] = across
        for at, line in enumerate(lines):
            self.table_v[at:at + 1, :] = jnp.zeros((1, T), jnp.int32) if line is None else line
        copy = pltpu.make_async_copy(self.table_v, self.table, self.local_sem.at[6])
        copy.start()
        for h in range(2):
            self.sums[h][0] = jnp.zeros((T, T), F32)
        copy.wait()

    def gather_tile(self, h, piece, i, j):
        tile = self.panel[h].at[self.near_tile(piece, OFFS[i], OFFS[j], self.core)]
        self.send(tile, tile, self.ap_sem.at[h, piece, i * 4 + j], self.partner())

    def gather_across(self, h, piece, i):
        tile = self.panel[h].at[self.near_tile(piece, OFFS[i], 0, self.core)]
        self.send(tile, tile, self.a_sem.at[h, piece, 4 + 4 * i], self.neighbour(1 - piece, 1))
        self.send(tile, tile, self.a_sem.at[h, piece, 5 + 4 * i], self.neighbour(1 - piece, -1))

    def gather_own(self, h):
        self.own[h].wait()
        for piece in range(2):
            tile = self.panel[h].at[self.near_tile(piece, 0, 0, self.core)]
            self.send(tile, tile, self.a_sem.at[h, piece, 0], self.neighbour(piece, 1))
            self.send(tile, tile, self.a_sem.at[h, piece, 1], self.neighbour(piece, -1))
        for piece in range(2):
            self.gather_across(h, piece, 0)
        for piece in range(2):
            self.gather_tile(h, piece, 0, 0)

    def gather_first(self, h):
        for i, rows, onward in ((1, 0, 1), (2, HALF, -1)):
            for piece in range(2):
                at = self.near_tile(piece, OFFS[i], 0, self.core)
                self.arrive(self.panel[h].at[at], self.a_sem.at[h, piece, i - 1])
                part = self.panel[h].at[at, pl.ds(rows, HALF)]
                self.send(part, part, self.a_sem.at[h, piece, i + 1], self.neighbour(piece, onward))
                self.gather_across(h, piece, i)
                self.gather_tile(h, piece, i, 0)

    def gather_second(self, h):
        for piece in range(2):
            at = self.near_tile(piece, 2, 0, self.core)
            self.arrive(self.panel[h].at[at, pl.ds(0, HALF)], self.a_sem.at[h, piece, 2])
            self.arrive(self.panel[h].at[at, pl.ds(HALF, HALF)], self.a_sem.at[h, piece, 3])
            self.gather_across(h, piece, 3)
            self.gather_tile(h, piece, 3, 0)

    def gather_third(self, h, which=(0, 1, 2, 3)):
        for i in which:
            for j, rows, onward in ((1, 0, 1), (2, HALF, -1)):
                for piece in range(2):
                    at = self.near_tile(piece, OFFS[i], OFFS[j], self.core)
                    self.arrive(self.panel[h].at[at], self.a_sem.at[h, piece, 4 + 4 * i + j - 1])
                    part = self.panel[h].at[at, pl.ds(rows, HALF)]
                    self.send(part, part, self.a_sem.at[h, piece, 4 + 4 * i + j + 1], self.neighbour(1 - piece, onward))
                    self.gather_tile(h, piece, i, j)

    def gather_fourth(self, h):
        for i in range(4):
            for piece in range(2):
                at = self.near_tile(piece, OFFS[i], 2, self.core)
                self.arrive(self.panel[h].at[at, pl.ds(0, HALF)], self.a_sem.at[h, piece, 4 + 4 * i + 2])
                self.arrive(self.panel[h].at[at, pl.ds(HALF, HALF)], self.a_sem.at[h, piece, 4 + 4 * i + 3])
                self.gather_tile(h, piece, i, 3)

    def gather_partner(self, h):
        for i in range(4):
            for j in range(4):
                for piece in range(2):
                    at = self.near_tile(piece, OFFS[i], OFFS[j], 1 - self.core)
                    self.arrive(self.panel[h].at[at], self.ap_sem.at[h, piece, i * 4 + j])

    def slots(self, h, prev, ids, source, dims):
        sums = self.sums[h]

        def block(at, carry):
            for u in range(UNROLL):
                k = at * UNROLL + u
                product = lax.dot_general(
                    self.tiles[k], source[self.table[ids, k]], (dims, ((), ())), preferred_element_type=F32)
                sums[k + 1] = sums[self.table[prev, k]] + product
            return carry

        lax.fori_loop(0, SLOTS // UNROLL, block, 0)

    def forward(self, h):
        self.slots(h, PREV_F, COL_ID, self.panel[h], ((1,), (0,)))

    def backward(self, h):
        self.slots(h, PREV_B, ROW_ID, self.ga[h], ((0,), (0,)))

    def row_sum(self, h, tile):
        return self.sums[h][self.table[LAST_F, tile]]

    def col_sum(self, h, tile):
        return self.sums[h][self.table[LAST_B, tile]]

    def reduce_step(self, h, step):
        for way in range(2):
            sign = 1 - 2 * way
            block = self.ring(sign * (4 - step))
            stage = self.zs.at[h, way, step]
            if step == 0:
                stage[way] = self.row_sum(h, block * 2 + way).astype(BF16)
                self.send(stage.at[way], self.zr.at[h, way, step, way], self.z_sem.at[h, way, step], (self.row, self.ring(sign)))
                continue
            got = self.zr.at[h, way, step - 1]
            self.arrive(got.at[way] if step == 1 else got, self.z_sem.at[h, way, step - 1])
            for piece in range(2):
                value = self.row_sum(h, block * 2 + piece)
                if step > 1 or piece == way:
                    value = value + got[piece].astype(F32)
                stage[piece] = value.astype(BF16)
            self.send(stage, self.zr.at[h, way, step], self.z_sem.at[h, way, step], (self.row, self.ring(sign)))

    def reduce_end(self, h):
        for way in range(2):
            self.arrive(self.zr.at[h, way, 3], self.z_sem.at[h, way, 3])
        for piece in range(2):
            value = self.row_sum(h, self.z * 2 + piece)
            value = value + self.zr[h, 0, 3, piece].astype(F32) + self.zr[h, 1, 3, piece].astype(F32)
            self.agg[pl.ds(piece * T, T), pl.ds(h * T, T)] = value.astype(BF16)

    def dense(self):
        for copy in self.dense_in:
            copy.wait()
        pre = jnp.dot(self.agg[...], self.weight_v[...], preferred_element_type=F32)
        result, slope = gelu_pair(pre)
        grad_pre = (self.cot_v[...].astype(F32) * slope).astype(BF16)
        self.hid_v[...] = result.astype(BF16)
        grad_agg = lax.dot_general(
            grad_pre, self.weight_v[...], (((1,), (1,)), ((), ())), preferred_element_type=F32).astype(BF16)
        for h in range(2):
            for piece in range(2):
                self.ga[h][self.z * 2 + piece] = grad_agg[piece * T:(piece + 1) * T, h * T:(h + 1) * T]
        self.spread_own(0)
        self.spread_own(1)
        total = lax.dot_general(
            self.agg[...], grad_pre, (((0,), (0,)), ((), ())), preferred_element_type=F32)
        self.wg[...] = total.reshape(32, 8, 256)
        self.hidden_out = pltpu.make_async_copy(self.hid_v, self.hidden, self.local_sem.at[7])
        self.hidden_out.start()

    def weight_copy(self, step):
        there = lax.rem(self.row + step, 32)
        return pltpu.make_async_remote_copy(
            src_ref=self.wg.at[there], dst_ref=self.wg_row.at[self.row], send_sem=self.wr_send.at[step],
            recv_sem=self.wr_recv.at[step], device_id=(there, self.z), device_id_type=MESH)

    def weight_start(self):
        def start(step, carry):
            self.weight_copy(step).start()
            return carry

        lax.fori_loop(1, 32, start, 0)

    def weight_column_copy(self, step):
        there = lax.rem(self.z + step, RING)
        return pltpu.make_async_remote_copy(
            src_ref=self.wg_part, dst_ref=self.wg_col.at[self.z], send_sem=self.wc_send.at[step],
            recv_sem=self.wc_recv.at[step], device_id=(self.row, there), device_id_type=MESH)

    def weight_middle(self):
        def wait(step, carry):
            came = lax.rem(self.row + 32 - step, 32)
            pltpu.make_async_remote_copy(
                src_ref=self.wg.at[came], dst_ref=self.wg_row.at[came], send_sem=self.wr_send.at[step],
                recv_sem=self.wr_recv.at[step], device_id=(came, self.z), device_id_type=MESH).wait_recv()
            return carry

        lax.fori_loop(1, 32, wait, 0)
        self.wg_row[self.row] = self.wg[self.row]
        part = jnp.sum(self.wg_row[...], axis=0)
        self.wg_part[...] = part
        self.wg_col[self.z] = part

        def start(step, carry):
            self.weight_column_copy(step).start()
            return carry

        lax.fori_loop(1, RING, start, 0)

    def weight_end(self):
        def wait(step, carry):
            came = lax.rem(self.z + RING - step, RING)
            pltpu.make_async_remote_copy(
                src_ref=self.wg_part, dst_ref=self.wg_col.at[came], send_sem=self.wc_send.at[step],
                recv_sem=self.wc_recv.at[step], device_id=(self.row, came), device_id_type=MESH).wait_recv()
            return carry

        lax.fori_loop(1, RING, wait, 0)
        self.wg_out[...] = jnp.sum(self.wg_col[...], axis=0)
        out = pltpu.make_async_copy(self.wg_out, self.weight_grad, self.local_sem.at[8])
        out.start()
        return out

    def spread_own(self, h):
        mine = self.ga[h].at[pl.ds(self.z * 2, 2)]
        for way in range(2):
            self.send(mine, mine, self.d_sem.at[h, way, 0], (self.row, self.ring(1 - 2 * way)))

    def spread_step(self, h, step):
        for way in range(2):
            sign = 1 - 2 * way
            first = self.ring(-sign * step) * 2
            if step == 4:
                self.arrive(self.ga[h].at[first + way], self.d_sem.at[h, way, 3])
                continue
            block = self.ga[h].at[pl.ds(first, 2)]
            self.arrive(block, self.d_sem.at[h, way, step - 1])
            onward = self.ga[h].at[first + way] if step == 3 else block
            self.send(onward, onward, self.d_sem.at[h, way, step], (self.row, self.ring(sign)))

    def grad_tile(self, h, piece, keep, step, core):
        return self.col_sum(h, self.tile_at(piece, keep, self.along(1 - piece, step), core))

    def grad_partner(self, h):
        for at, step in enumerate((2, 1, -1, 0)):
            for piece in range(2):
                for keep in range(SIDE):
                    self.ps[h, piece, at, keep] = self.grad_tile(h, piece, keep, step, 1 - self.core).astype(BF16)
                self.send(self.ps.at[h, piece, at], self.pr.at[h, piece, at], self.p_sem.at[h, piece, at], self.partner())

    def chip_tile(self, h, piece, at, keep):
        step = (2, 1, -1, 0)[at]
        return self.grad_tile(h, piece, keep, step, self.core) + self.pr[h, piece, at, keep].astype(F32)

    def grad_first(self, h):
        for piece in range(2):
            self.arrive(self.pr.at[h, piece, 0], self.p_sem.at[h, piece, 0])
            for keep in range(SIDE):
                self.s1[h, piece, keep] = self.chip_tile(h, piece, 0, keep).astype(BF16)
            for way in range(2):
                self.send(
                    self.s1.at[h, piece, :, pl.ds(way * HALF, HALF)], self.r1.at[h, piece, way],
                    self.r1_sem.at[h, piece, way], self.neighbour(1 - piece, 1 - 2 * way))

    def grad_second(self, h):
        for piece in range(2):
            for way in range(2):
                self.arrive(self.pr.at[h, piece, 1 + way], self.p_sem.at[h, piece, 1 + way])
                self.arrive(self.r1.at[h, piece, way], self.r1_sem.at[h, piece, way])
                for keep in range(SIDE):
                    value = self.chip_tile(h, piece, 1 + way, keep)
                    added = value[way * HALF:(way + 1) * HALF] + self.r1[h, piece, way, keep].astype(F32)
                    plain = value[(1 - way) * HALF:(2 - way) * HALF]
                    self.s2[h, piece, way, keep, pl.ds(way * HALF, HALF)] = added.astype(BF16)
                    self.s2[h, piece, way, keep, pl.ds((1 - way) * HALF, HALF)] = plain.astype(BF16)
                self.send(
                    self.s2.at[h, piece, way], self.r2.at[h, piece, way],
                    self.r2_sem.at[h, piece, way], self.neighbour(1 - piece, 1 - 2 * way))

    def grad_third(self, h):
        for piece in range(2):
            self.arrive(self.pr.at[h, piece, 3], self.p_sem.at[h, piece, 3])
            for way in range(2):
                self.arrive(self.r2.at[h, piece, way], self.r2_sem.at[h, piece, way])
            for keep in range(SIDE):
                value = self.chip_tile(h, piece, 3, keep)
                value = value + self.r2[h, piece, 0, keep].astype(F32) + self.r2[h, piece, 1, keep].astype(F32)
                self.axis_sum[h, piece, keep] = value
            self.s3[h, piece] = self.axis_sum[h, piece, self.along(piece, 2)].astype(BF16)
            for way in range(2):
                self.send(
                    self.s3.at[h, piece, pl.ds(way * HALF, HALF)], self.r3.at[h, piece, way],
                    self.r3_sem.at[h, piece, way], self.neighbour(piece, 1 - 2 * way))

    def grad_fourth(self, h):
        for piece in range(2):
            for way in range(2):
                sign = 1 - 2 * way
                self.arrive(self.r3.at[h, piece, way], self.r3_sem.at[h, piece, way])
                value = self.axis_sum[h, piece, self.along(piece, sign)]
                added = value[way * HALF:(way + 1) * HALF] + self.r3[h, piece, way].astype(F32)
                plain = value[(1 - way) * HALF:(2 - way) * HALF]
                self.s4[h, piece, way, pl.ds(way * HALF, HALF)] = added.astype(BF16)
                self.s4[h, piece, way, pl.ds((1 - way) * HALF, HALF)] = plain.astype(BF16)
                self.send(
                    self.s4.at[h, piece, way], self.r4.at[h, piece, way],
                    self.r4_sem.at[h, piece, way], self.neighbour(piece, sign))

    def grad_end(self, h):
        for piece in range(2):
            for way in range(2):
                self.arrive(self.r4.at[h, piece, way], self.r4_sem.at[h, piece, way])
            value = self.axis_sum[h, piece, self.at[piece]]
            value = value + self.r4[h, piece, 0].astype(F32) + self.r4[h, piece, 1].astype(F32)
            self.fg_v[pl.ds(piece * T, T), pl.ds(h * T, T)] = value

    def finish(self):
        out = pltpu.make_async_copy(self.fg_v, self.feature_grad, self.local_sem.at[9])
        out.start()
        weight_out = self.weight_end()
        self.hidden_out.wait()
        for copy in self.sends:
            copy.wait_send()

        def drain_row(step, carry):
            self.weight_copy(step).wait_send()
            return carry

        def drain_column(step, carry):
            self.weight_column_copy(step).wait_send()
            return carry

        lax.fori_loop(1, 32, drain_row, 0)
        lax.fori_loop(1, RING, drain_column, 0)
        weight_out.wait()
        out.wait()

    def run(self):
        self.greet()
        self.load()
        self.index_table()
        self.met()
        self.gather_own(0)
        self.gather_own(1)
        self.gather_first(0)
        self.gather_second(0)
        self.gather_first(1)
        self.gather_third(0)
        self.gather_second(1)
        self.gather_fourth(0)
        self.gather_partner(0)
        self.tiles_in.wait()
        self.forward(0)
        self.reduce_step(0, 0)
        self.gather_third(1)
        self.gather_fourth(1)
        self.reduce_step(0, 1)
        self.gather_partner(1)
        self.forward(1)
        self.reduce_step(1, 0)
        self.reduce_step(0, 2)
        self.reduce_step(1, 1)
        self.reduce_step(0, 3)
        self.reduce_step(1, 2)
        self.reduce_end(0)
        self.reduce_step(1, 3)
        self.reduce_end(1)
        self.dense()
        self.weight_start()
        self.spread_step(0, 1)
        self.spread_step(1, 1)
        self.spread_step(0, 2)
        self.spread_step(1, 2)
        self.spread_step(0, 3)
        self.spread_step(0, 4)
        self.spread_step(1, 3)
        self.backward(0)
        self.grad_partner(0)
        self.spread_step(1, 4)
        self.grad_first(0)
        self.backward(1)
        self.grad_partner(1)
        self.grad_second(0)
        self.grad_first(1)
        self.weight_middle()
        self.grad_third(0)
        self.grad_second(1)
        self.grad_fourth(0)
        self.grad_third(1)
        self.grad_end(0)
        self.grad_fourth(1)
        self.grad_end(1)
        self.finish()


def kernel(names, *refs):
    count, features, weight, tile_values, coords, cotangent, hidden, weight_grad, feature_grad = refs[:9]
    named = dict(zip(names, refs[9:]))
    Layer(count, features, weight, tile_values, coords, cotangent, hidden, weight_grad, feature_grad, named).run()


def per_device(features, weight, tile_values, tile_coords, tile_count, cotangent):
    buffers = scratch()
    anywhere = pl.BlockSpec(memory_space=pl.ANY)
    return pl.pallas_call(
        functools.partial(kernel, tuple(buffers)),
        out_shape=(
            jax.ShapeDtypeStruct((256, 256), BF16),
            jax.ShapeDtypeStruct((8, 256), F32),
            jax.ShapeDtypeStruct((256, 256), F32),
        ),
        in_specs=[pl.BlockSpec(memory_space=pltpu.SMEM)] + [anywhere] * 5,
        out_specs=(anywhere, anywhere, anywhere),
        scratch_shapes=list(buffers.values()),
        compiler_params=pltpu.CompilerParams(
            collective_id=0, has_side_effects=True, vmem_limit_bytes=60 * 1024 * 1024),
        name="graph_layer",
    )(tile_count, features.reshape(2, 128, 256), weight, tile_values, tile_coords, cotangent)


def solution(mesh):
    return jax.shard_map(
        per_device,
        mesh=mesh,
        in_specs=(
            P(("row", "col"), None),
            P(),
            P(("row", "col"), None, None),
            P(("row", "col"), None),
            P(("row", "col")),
            P(("row", "col"), None),
        ),
        out_specs=(P(("row", "col"), None), P("row", None), P(("row", "col"), None)),
        check_vma=False,
    )
```

```python
import functools

import jax
import jax.numpy as jnp
from jax import lax
from jax.experimental import pallas as pl
from jax.experimental.pallas import tpu as pltpu
from jax.sharding import PartitionSpec as P

gelu_scale = 0.7978845608028654
gelu_cubic = 0.044715

MESH = pl.DeviceIdType.MESH
BF16 = jnp.bfloat16
F32 = jnp.float32
T = 128
SIDE = 4
RING = 8
SLOTS = 96
ROW_TILES = 16
COL_TILES = 64
UNROLL = 16

PREV_F, LAST_F, PREV_B, LAST_B, ROW_ID, PANEL_ID = range(6)

OTHERS = (2, 1, -1)


def gelu_pair(values):
    inner = gelu_scale * (values + gelu_cubic * values * values * values)
    slope_tanh = jnp.tanh(inner)
    result = 0.5 * values * (1.0 + slope_tanh)
    slope = 0.5 * (1.0 + slope_tanh) + 0.5 * values * (
        1.0 - slope_tanh * slope_tanh
    ) * gelu_scale * (1.0 + 3.0 * gelu_cubic * values * values)
    return (result, slope)


def scratch():
    dma = pltpu.SemaphoreType.DMA
    return {
        "tiles": pltpu.VMEM((SLOTS, T, T), BF16),
        "weight_v": pltpu.VMEM((256, 256), BF16),
        "cot_v": pltpu.VMEM((256, 256), BF16),
        "coords_v": pltpu.VMEM((2, SLOTS), jnp.int32),
        "table_v": pltpu.VMEM((8, SLOTS), jnp.int32),
        "table": pltpu.SMEM((8, SLOTS), jnp.int32),
        "panel0": pltpu.VMEM((COL_TILES, T, T), BF16),
        "panel1": pltpu.VMEM((COL_TILES, T, T), BF16),
        "sums0": pltpu.VMEM((SLOTS + 1, T, T), F32),
        "sums1": pltpu.VMEM((SLOTS + 1, T, T), F32),
        "zs": pltpu.VMEM((2, 2, 2, 4, T, T), BF16),
        "zr": pltpu.VMEM((2, 2, 2, 4, T, T), BF16),
        "agg": pltpu.VMEM((256, 256), BF16),
        "grad_pre": pltpu.VMEM((256, 256), BF16),
        "hid_v": pltpu.VMEM((256, 256), BF16),
        "wg": pltpu.VMEM((32, 8, 256), F32),
        "wg_row": pltpu.VMEM((32, 8, 256), F32),
        "wg_part": pltpu.VMEM((8, 256), F32),
        "wg_col": pltpu.VMEM((8, 8, 256), F32),
        "wg_out": pltpu.VMEM((8, 256), F32),
        "ga0": pltpu.VMEM((ROW_TILES, T, T), BF16),
        "ga1": pltpu.VMEM((ROW_TILES, T, T), BF16),
        "ps": pltpu.VMEM((2, 4, 2, SIDE, T, T), BF16),
        "pr": pltpu.VMEM((2, 4, 2, SIDE, T, T), BF16),
        "s1": pltpu.VMEM((2, 2, 3, SIDE, T, T), BF16),
        "r1": pltpu.VMEM((2, 2, 3, SIDE, T, T), BF16),
        "axis_sum": pltpu.VMEM((2, 2, SIDE, T, T), F32),
        "s2": pltpu.VMEM((2, 2, 3, T, T), BF16),
        "r2": pltpu.VMEM((2, 2, 3, T, T), BF16),
        "fg_v": pltpu.VMEM((256, 256), F32),
        "own_sem": dma((2,)),
        "in_sem": dma((5,)),
        "out_sem": dma((3,)),
        "a_send": dma((2,)),
        "a1_sem": dma((2, 2, 3)),
        "a2_sem": dma((2, 2, 4)),
        "ap_sem": dma((2,)),
        "z_send": dma((1,)),
        "z_sem": dma((2, 2, 2, 4)),
        "d_send": dma((1,)),
        "d_sem": dma((2, 2, 2, 4)),
        "e_send": dma((2,)),
        "p_sem": dma((2, 4)),
        "r1_sem": dma((2, 2)),
        "r2_sem": dma((2, 2)),
        "w_sem": dma((4,)),
    }


class Layer:
    def __init__(self, operands, results, refs):
        self.__dict__.update(refs)
        self.count, self.features, self.weight, self.tile_values, self.coords, self.cotangent = operands
        self.hidden, self.weight_grad, self.feature_grad = results
        self.panel = (self.panel0, self.panel1)
        self.sums = (self.sums0, self.sums1)
        self.ga = (self.ga0, self.ga1)
        self.row = lax.axis_index("row")
        self.z = lax.axis_index("col")
        self.core = lax.rem(self.row, 2)
        self.at = (self.row // 8, lax.rem(self.row // 2, SIDE))

    def along(self, axis, step):
        return lax.rem(self.at[axis] + step % SIDE, SIDE)

    def neighbour(self, axis, step):
        spot = [self.at[0], self.at[1]]
        spot[axis] = self.along(axis, step)
        return ((spot[0] * SIDE + spot[1]) * 2 + self.core, self.z)

    def partner(self):
        return (self.row + 1 - 2 * self.core, self.z)

    def ring(self, step):
        return lax.rem(self.z + step % RING, RING)

    def ring_device(self, way):
        return (self.row, self.ring(1 - 2 * way))

    def panel_at(self, piece, first, second, core):
        return ((piece * 2 + core) * SIDE + first) * SIDE + second

    def send(self, src, dst, send_sem, recv_sem, device):
        pltpu.make_async_remote_copy(
            src_ref=src, dst_ref=dst, send_sem=send_sem, recv_sem=recv_sem,
            device_id=device, device_id_type=MESH,
        ).start()

    def landed(self, ref, sem):
        pltpu.make_async_copy(ref, ref, sem).wait()

    def load(self):
        self.own = []
        for h in range(2):
            for piece in range(2):
                at = self.panel_at(piece, self.at[piece], self.at[1 - piece], self.core)
                copy = pltpu.make_async_copy(
                    self.features.at[pl.ds(piece * T, T), pl.ds(h * T, T)], self.panel[h].at[at], self.own_sem.at[h])
                copy.start()
        sem = self.in_sem
        self.coords_in = pltpu.make_async_copy(self.coords, self.coords_v, sem.at[0])
        self.tiles_in = pltpu.make_async_copy(self.tile_values, self.tiles, sem.at[1])
        self.dense_in = (
            pltpu.make_async_copy(self.weight, self.weight_v, sem.at[2]),
            pltpu.make_async_copy(self.cotangent, self.cot_v, sem.at[3]),
        )
        for copy in (self.coords_in, self.tiles_in, *self.dense_in):
            copy.start()

    def greet(self):
        barrier = pltpu.get_barrier_semaphore()
        for device in self.friends():
            pl.semaphore_signal(barrier, inc=1, device_id=device, device_id_type=MESH)

    def friends(self):
        around = [self.neighbour(axis, step) for axis in range(2) for step in OTHERS]
        return [self.partner(), self.ring_device(0), self.ring_device(1)] + around

    def met(self):
        pl.semaphore_wait(pltpu.get_barrier_semaphore(), 9)

    def index_table(self):
        self.coords_in.wait()
        slot = lax.broadcasted_iota(jnp.int32, (SLOTS, SLOTS), 0)
        lane = lax.broadcasted_iota(jnp.int32, (SLOTS, SLOTS), 1)
        live = slot < self.count[0]
        lines = [None] * 8
        for column, prev, last in ((0, PREV_F, LAST_F), (1, PREV_B, LAST_B)):
            across = self.coords_v[column:column + 1, :]
            down = jnp.sum(jnp.where(slot == lane, across, 0), axis=1, keepdims=True)
            earlier = live & (slot < lane) & (down == across)
            lines[prev] = jnp.max(jnp.where(earlier, slot + 1, 0), axis=0, keepdims=True)
            lines[last] = jnp.max(jnp.where(live & (down == lane), slot + 1, 0), axis=0, keepdims=True)
            if column == 0:
                lines[ROW_ID] = across
            else:
                x, y, core, piece = across // 16, (across // 4) % 4, (across // 2) % 2, across % 2
                straight = piece == 0
                lines[PANEL_ID] = self.panel_at(piece, jnp.where(straight, x, y), jnp.where(straight, y, x), core)
        for at, line in enumerate(lines):
            self.table_v[at:at + 1, :] = jnp.zeros((1, SLOTS), jnp.int32) if line is None else line
        copy = pltpu.make_async_copy(self.table_v, self.table, self.in_sem.at[4])
        copy.start()
        for h in range(2):
            self.sums[h][0] = jnp.zeros((T, T), F32)
        copy.wait()

    def gather_across(self, h, piece, step1):
        first = self.along(piece, step1)
        at = self.panel_at(piece, first, self.at[1 - piece], self.core)
        tile = self.panel[h].at[at]
        for step in OTHERS:
            self.send(tile, tile, self.a_send.at[h], self.a2_sem.at[h, piece, step1 % SIDE], self.neighbour(1 - piece, step))

    def gather_own(self, h):
        self.landed(self.panel[h].at[pl.ds(0, 2)], self.own_sem.at[h])
        for piece in range(2):
            at = self.panel_at(piece, self.at[piece], self.at[1 - piece], self.core)
            tile = self.panel[h].at[at]
            for step in OTHERS:
                self.send(tile, tile, self.a_send.at[h], self.a1_sem.at[h, piece, step % SIDE - 1], self.neighbour(piece, step))
        for piece in range(2):
            self.gather_across(h, piece, 0)

    def gather_first(self, h):
        for step in (1, -1, 2):
            for piece in range(2):
                came = self.panel_at(piece, self.along(piece, -step), self.at[1 - piece], self.core)
                self.landed(self.panel[h].at[came], self.a1_sem.at[h, piece, step % SIDE - 1])
                self.gather_across(h, piece, -step)

    def gather_second(self, h):
        for step1 in (0, -1, 1, 2):
            for piece in range(2):
                first = self.panel_at(piece, self.along(piece, step1), 0, self.core)
                self.landed(self.panel[h].at[pl.ds(first, 3)], self.a2_sem.at[h, piece, step1 % SIDE])
                line = self.panel[h].at[pl.ds(first, SIDE)]
                self.send(line, line, self.a_send.at[h], self.ap_sem.at[h], self.partner())

    def gather_partner(self, h):
        self.landed(self.panel[h].at[pl.ds(0, 32)], self.ap_sem.at[h])

    def forward(self, h):
        sums, panel = self.sums[h], self.panel[h]

        def block(at, carry):
            for u in range(UNROLL):
                k = at * UNROLL + u
                product = jnp.dot(self.tiles[k], panel[self.table[PANEL_ID, k]], preferred_element_type=F32)
                sums[k + 1] = sums[self.table[PREV_F, k]] + product
            return carry

        lax.fori_loop(0, SLOTS // UNROLL, block, 0)

    def backward(self, h):
        sums, ga = self.sums[h], self.ga[h]

        def block(at, carry):
            for u in range(UNROLL):
                k = at * UNROLL + u
                product = jnp.dot(ga[self.table[ROW_ID, k]], self.tiles[k], preferred_element_type=F32)
                sums[k + 1] = sums[self.table[PREV_B, k]] + product
            return carry

        lax.fori_loop(0, SLOTS // UNROLL, block, 0)

    def reduce_step(self, h, piece, step):
        for way in range(2):
            if step == 0 and way != piece:
                continue
            sign = 1 - 2 * way
            block = self.ring(sign * (4 - step))
            value = self.sums[h][self.table[LAST_F, block * 2 + piece]]
            if step > 1 or (step == 1 and way == piece):
                self.landed(self.zr.at[h, piece, way, step - 1], self.z_sem.at[h, piece, way, step - 1])
                value = value + self.zr[h, piece, way, step - 1].astype(F32)
            self.zs[h, piece, way, step] = value.astype(BF16)
            self.send(
                self.zs.at[h, piece, way, step], self.zr.at[h, piece, way, step], self.z_send.at[0],
                self.z_sem.at[h, piece, way, step], self.ring_device(way))

    def reduce_end(self, h, piece):
        value = self.sums[h][self.table[LAST_F, self.z * 2 + piece]]
        for way in range(2):
            self.landed(self.zr.at[h, piece, way, 3], self.z_sem.at[h, piece, way, 3])
            value = value + self.zr[h, piece, way, 3].astype(F32)
        self.agg[piece * T:(piece + 1) * T, h * T:(h + 1) * T] = value.astype(BF16)

    def dense(self, piece):
        rows = slice(piece * T, (piece + 1) * T)
        if piece == 0:
            for copy in self.dense_in:
                copy.wait()
        pre = jnp.dot(self.agg[rows, :], self.weight_v[...], preferred_element_type=F32)
        result, slope = gelu_pair(pre)
        grad_pre = (self.cot_v[rows, :].astype(F32) * slope).astype(BF16)
        turned = lax.dot_general(
            self.weight_v[...], grad_pre, (((1,), (1,)), ((), ())), preferred_element_type=F32).astype(BF16)
        for h in range(2):
            self.ga[h][self.z * 2 + piece] = turned[h * T:(h + 1) * T]
        self.hid_v[rows, :] = result.astype(BF16)
        self.grad_pre[rows, :] = grad_pre
        for h in range(2):
            mine = self.ga[h].at[self.z * 2 + piece]
            for way in range(2):
                self.send(mine, mine, self.d_send.at[0], self.d_sem.at[h, piece, way, 0], self.ring_device(way))

    def weight_start(self):
        self.hidden_out = pltpu.make_async_copy(self.hid_v, self.hidden, self.out_sem.at[0])
        self.hidden_out.start()
        total = lax.dot_general(
            self.agg[...], self.grad_pre[...], (((0,), (0,)), ((), ())), preferred_element_type=F32)
        self.wg[...] = total.reshape(32, 8, 256)

        def start(step, carry):
            there = lax.rem(self.row + step, 32)
            self.send(self.wg.at[there], self.wg_row.at[self.row], self.w_sem.at[0], self.w_sem.at[1], (there, self.z))
            return carry

        lax.fori_loop(1, 32, start, 0)

    def weight_middle(self):
        self.landed(self.wg_row.at[pl.ds(0, 31)], self.w_sem.at[1])
        self.wg_row[self.row] = self.wg[self.row]
        part = jnp.sum(self.wg_row[...], axis=0)
        self.wg_part[...] = part
        self.wg_col[self.z] = part

        def start(step, carry):
            there = lax.rem(self.z + step, RING)
            self.send(self.wg_part, self.wg_col.at[self.z], self.w_sem.at[2], self.w_sem.at[3], (self.row, there))
            return carry

        lax.fori_loop(1, RING, start, 0)

    def weight_end(self):
        self.landed(self.wg_col.at[pl.ds(0, 7)], self.w_sem.at[3])
        self.wg_out[...] = jnp.sum(self.wg_col[...], axis=0)
        self.weight_out = pltpu.make_async_copy(self.wg_out, self.weight_grad, self.out_sem.at[1])
        self.weight_out.start()

    def spread_step(self, h, piece, step):
        for way in range(2):
            if step == 4 and way != piece:
                continue
            tile = self.ga[h].at[self.ring((2 * way - 1) * step) * 2 + piece]
            self.landed(tile, self.d_sem.at[h, piece, way, step - 1])
            if step < 3 or (step == 3 and way == piece):
                self.send(tile, tile, self.d_send.at[0], self.d_sem.at[h, piece, way, step], self.ring_device(way))

    def grad_tile(self, h, piece, keep, step, core):
        reduce = self.along(1 - piece, step)
        x, y = (keep, reduce) if piece == 0 else (reduce, keep)
        return self.sums[h][self.table[LAST_B, ((x * SIDE + y) * 2 + core) * 2 + piece]]

    def grad_partner(self, h):
        for at, step in enumerate((*OTHERS, 0)):
            for piece in range(2):
                for keep in range(SIDE):
                    self.ps[h, at, piece, keep] = self.grad_tile(h, piece, keep, step, 1 - self.core).astype(BF16)
            self.send(self.ps.at[h, at], self.pr.at[h, at], self.e_send.at[h], self.p_sem.at[h, at], self.partner())

    def chip_tile(self, h, at, piece, keep):
        step = (*OTHERS, 0)[at]
        return self.grad_tile(h, piece, keep, step, self.core) + self.pr[h, at, piece, keep].astype(F32)

    def grad_first(self, h):
        for at, step in enumerate(OTHERS):
            self.landed(self.pr.at[h, at], self.p_sem.at[h, at])
            for piece in range(2):
                for keep in range(SIDE):
                    self.s1[h, piece, at, keep] = self.chip_tile(h, at, piece, keep).astype(BF16)
                self.send(
                    self.s1.at[h, piece, at], self.r1.at[h, piece, at], self.e_send.at[h],
                    self.r1_sem.at[h, piece], self.neighbour(1 - piece, step))

    def grad_second(self, h):
        self.landed(self.pr.at[h, 3], self.p_sem.at[h, 3])
        for piece in range(2):
            self.landed(self.r1.at[h, piece], self.r1_sem.at[h, piece])
            for keep in range(SIDE):
                value = self.chip_tile(h, 3, piece, keep)
                for at in range(3):
                    value = value + self.r1[h, piece, at, keep].astype(F32)
                self.axis_sum[h, piece, keep] = value
            for at, step in enumerate(OTHERS):
                self.s2[h, piece, at] = self.axis_sum[h, piece, self.along(piece, step)].astype(BF16)
                self.send(
                    self.s2.at[h, piece, at], self.r2.at[h, piece, at], self.e_send.at[h],
                    self.r2_sem.at[h, piece], self.neighbour(piece, step))

    def grad_end(self, h):
        for piece in range(2):
            self.landed(self.r2.at[h, piece], self.r2_sem.at[h, piece])
            value = self.axis_sum[h, piece, self.at[piece]]
            for at in range(3):
                value = value + self.r2[h, piece, at].astype(F32)
            self.fg_v[piece * T:(piece + 1) * T, h * T:(h + 1) * T] = value.T

    def finish(self):
        out = pltpu.make_async_copy(self.fg_v, self.feature_grad, self.out_sem.at[2])
        out.start()
        self.drain()
        self.landed(self.wg_row.at[pl.ds(0, 31)], self.w_sem.at[0])
        self.landed(self.wg_col.at[pl.ds(0, 7)], self.w_sem.at[2])
        self.hidden_out.wait()
        self.weight_out.wait()
        out.wait()

    def drain(self, stages="azde"):
        some = self.panel0
        if "a" in stages:
            for h in range(2):
                self.landed(some.at[pl.ds(0, 62)], self.a_send.at[h])
        if "z" in stages:
            self.landed(some.at[pl.ds(0, 28)], self.z_send.at[0])
        if "d" in stages:
            self.landed(some.at[pl.ds(0, 28)], self.d_send.at[0])
        if "e" in stages:
            for h in range(2):
                self.landed(some.at[pl.ds(0, 62)], self.e_send.at[h])

    def run(self):
        self.greet()
        self.load()
        self.met()
        self.gather_own(0)
        self.gather_own(1)
        self.index_table()
        self.gather_first(0)
        self.gather_first(1)
        self.gather_second(0)
        self.gather_partner(0)
        self.tiles_in.wait()
        self.forward(0)
        for piece in range(2):
            self.reduce_step(0, piece, 0)
        self.gather_second(1)
        for piece in range(2):
            self.reduce_step(0, piece, 1)
        self.gather_partner(1)
        self.forward(1)
        for piece in range(2):
            self.reduce_step(1, piece, 0)
        for piece in range(2):
            self.reduce_step(1, piece, 1)
            self.reduce_step(0, piece, 2)
        for piece in range(2):
            self.reduce_step(1, piece, 2)
            self.reduce_step(0, piece, 3)
        for piece in range(2):
            self.reduce_step(1, piece, 3)
            self.reduce_end(0, piece)
        self.reduce_end(1, 0)
        self.dense(0)
        self.reduce_end(1, 1)
        self.dense(1)
        self.weight_start()
        for step in (1, 2, 3):
            for piece in range(2):
                for h in range(2):
                    self.spread_step(h, piece, step)
        for piece in range(2):
            self.spread_step(0, piece, 4)
        self.backward(0)
        self.grad_partner(0)
        for piece in range(2):
            self.spread_step(1, piece, 4)
        self.grad_first(0)
        self.backward(1)
        self.grad_partner(1)
        self.grad_second(0)
        self.grad_first(1)
        self.weight_middle()
        self.grad_second(1)
        self.grad_end(0)
        self.weight_end()
        self.grad_end(1)
        self.finish()


def kernel(names, *refs):
    Layer(refs[:6], refs[6:9], dict(zip(names, refs[9:]))).run()


def hand_over(*refs):
    for source, target in zip(refs[:3], refs[3:]):
        target[...] = source[...]


def per_device(features, weight, tile_values, tile_coords, tile_count, cotangent):
    buffers = scratch()
    anywhere = pl.BlockSpec(memory_space=pl.ANY)
    shapes = (
        jax.ShapeDtypeStruct((256, 256), BF16),
        jax.ShapeDtypeStruct((8, 256), F32),
        jax.ShapeDtypeStruct((256, 256), F32),
    )
    results = pl.pallas_call(
        functools.partial(kernel, tuple(buffers)),
        out_shape=shapes,
        in_specs=[pl.BlockSpec(memory_space=pltpu.SMEM)] + [anywhere] * 5,
        out_specs=(anywhere, anywhere, anywhere),
        scratch_shapes=list(buffers.values()),
        compiler_params=pltpu.CompilerParams(
            collective_id=0, has_side_effects=True, vmem_limit_bytes=60 * 1024 * 1024),
        name="graph_layer",
    )(tile_count, features, weight, tile_values, tile_coords.T, cotangent)
    whole = pl.BlockSpec(memory_space=pltpu.VMEM)
    return pl.pallas_call(
        hand_over, out_shape=shapes, in_specs=[whole] * 3, out_specs=(whole, whole, whole), name="hand_over",
    )(*results)


def solution(mesh):
    return jax.shard_map(
        per_device,
        mesh=mesh,
        in_specs=(
            P(("row", "col"), None),
            P(),
            P(("row", "col"), None, None),
            P(("row", "col"), None),
            P(("row", "col")),
            P(("row", "col"), None),
        ),
        out_specs=(P(("row", "col"), None), P("row", None), P(("row", "col"), None)),
        check_vma=False,
    )
```

```python
import functools

import jax
import jax.numpy as jnp
from jax import lax
from jax.experimental import pallas as pl
from jax.experimental.pallas import tpu as pltpu
from jax.sharding import PartitionSpec as P

gelu_scale = 0.7978845608028654
gelu_cubic = 0.044715

MESH = pl.DeviceIdType.MESH
BF16 = jnp.bfloat16
F32 = jnp.float32
T = 128
SIDE = 4
RING = 8
SLOTS = 96
ROW_TILES = 16
COL_TILES = 64
UNROLL = 16

PREV_F, LAST_F, PREV_B, LAST_B, ROW_ID, PANEL_ID = range(6)

OTHERS = (2, 1, -1)
LINES = (2, 1, -1, 0)


def gelu_pair(values):
    inner = gelu_scale * (values + gelu_cubic * values * values * values)
    slope_tanh = jnp.tanh(inner)
    result = 0.5 * values * (1.0 + slope_tanh)
    slope = 0.5 * (1.0 + slope_tanh) + 0.5 * values * (
        1.0 - slope_tanh * slope_tanh
    ) * gelu_scale * (1.0 + 3.0 * gelu_cubic * values * values)
    return (result, slope)


def scratch():
    dma = pltpu.SemaphoreType.DMA
    return {
        "tiles": pltpu.VMEM((SLOTS, T, T), BF16),
        "weight_v": pltpu.VMEM((256, 256), BF16),
        "cot_v": pltpu.VMEM((256, 256), BF16),
        "coords_v": pltpu.VMEM((2, SLOTS), jnp.int32),
        "table_v": pltpu.VMEM((8, SLOTS), jnp.int32),
        "table": pltpu.SMEM((8, SLOTS), jnp.int32),
        "panel0": pltpu.VMEM((COL_TILES, T, T), BF16),
        "panel1": pltpu.VMEM((COL_TILES, T, T), BF16),
        "sums0": pltpu.VMEM((SLOTS + 1, T, T), F32),
        "sums1": pltpu.VMEM((SLOTS + 1, T, T), F32),
        "zs": pltpu.VMEM((2, 2, 2, 4, T, T), BF16),
        "zm": pltpu.VMEM((2, 2, 2, 2, T, T), BF16),
        "zr": pltpu.VMEM((2, 2, 4, T, T), BF16),
        "agg": pltpu.VMEM((256, 256), BF16),
        "grad_pre": pltpu.VMEM((256, 256), BF16),
        "hid_v": pltpu.VMEM((256, 256), BF16),
        "wg": pltpu.VMEM((32, 8, 256), F32),
        "wg_row": pltpu.VMEM((32, 8, 256), F32),
        "wg_part": pltpu.VMEM((8, 256), F32),
        "wg_col": pltpu.VMEM((8, 8, 256), F32),
        "wg_out": pltpu.VMEM((8, 256), F32),
        "ga0": pltpu.VMEM((ROW_TILES, T, T), BF16),
        "ga1": pltpu.VMEM((ROW_TILES, T, T), BF16),
        "ps": pltpu.VMEM((2, SIDE, 2, SIDE, T, T), BF16),
        "pr": pltpu.VMEM((2, SIDE, 2, SIDE, T, T), BF16),
        "s1": pltpu.VMEM((2, 2, SIDE, 3, T, T), BF16),
        "r1": pltpu.VMEM((2, 2, SIDE, 3, T, T), BF16),
        "axis_sum": pltpu.VMEM((2, 2, T, T), F32),
        "s2": pltpu.VMEM((2, 2, 3, T, T), BF16),
        "r2": pltpu.VMEM((2, 2, 3, T, T), BF16),
        "fg_v": pltpu.VMEM((256, 256), F32),
        "own_sem": dma((2,)),
        "in_sem": dma((5,)),
        "out_sem": dma((3,)),
        "a_send": dma((2,)),
        "a1_sem": dma((2, 2, 3)),
        "a2_sem": dma((2, 2, 4)),
        "ap_sem": dma((2,)),
        "z_send": dma((1,)),
        "zm_sem": dma((2, 2, 2)),
        "zr_sem": dma((2, 2)),
        "d_send": dma((1,)),
        "dm_sem": dma((2, 2, 2)),
        "dr_sem": dma((2, 2)),
        "e_send": dma((2,)),
        "p_sem": dma((2, 4)),
        "r1_sem": dma((2, 2, SIDE)),
        "r2_sem": dma((2, 2)),
        "w_sem": dma((4,)),
    }


class Layer:
    def __init__(self, operands, results, refs):
        self.__dict__.update(refs)
        self.count, self.features, self.weight, self.tile_values, self.coords, self.cotangent = operands
        self.hidden, self.weight_grad, self.feature_grad = results
        self.panel = (self.panel0, self.panel1)
        self.sums = (self.sums0, self.sums1)
        self.ga = (self.ga0, self.ga1)
        self.row = lax.axis_index("row")
        self.z = lax.axis_index("col")
        self.core = lax.rem(self.row, 2)
        self.at = (self.row // 8, lax.rem(self.row // 2, SIDE))

    def along(self, axis, step):
        return lax.rem(self.at[axis] + step % SIDE, SIDE)

    def neighbour(self, axis, step):
        spot = [self.at[0], self.at[1]]
        spot[axis] = self.along(axis, step)
        return ((spot[0] * SIDE + spot[1]) * 2 + self.core, self.z)

    def partner(self):
        return (self.row + 1 - 2 * self.core, self.z)

    def ring(self, step):
        return lax.rem(self.z + step % RING, RING)

    def ring_device(self, step):
        return (self.row, self.ring(step))

    def panel_at(self, piece, first, second, core):
        return ((piece * 2 + core) * SIDE + first) * SIDE + second

    def send(self, src, dst, send_sem, recv_sem, device):
        pltpu.make_async_remote_copy(
            src_ref=src, dst_ref=dst, send_sem=send_sem, recv_sem=recv_sem,
            device_id=device, device_id_type=MESH,
        ).start()

    def landed(self, ref, sem):
        pltpu.make_async_copy(ref, ref, sem).wait()

    def load(self):
        self.own = []
        for h in range(2):
            for piece in range(2):
                at = self.panel_at(piece, self.at[piece], self.at[1 - piece], self.core)
                copy = pltpu.make_async_copy(
                    self.features.at[pl.ds(piece * T, T), pl.ds(h * T, T)], self.panel[h].at[at], self.own_sem.at[h])
                copy.start()
        sem = self.in_sem
        self.coords_in = pltpu.make_async_copy(self.coords, self.coords_v, sem.at[0])
        self.tiles_in = pltpu.make_async_copy(self.tile_values, self.tiles, sem.at[1])
        self.dense_in = (
            pltpu.make_async_copy(self.weight, self.weight_v, sem.at[2]),
            pltpu.make_async_copy(self.cotangent, self.cot_v, sem.at[3]),
        )
        for copy in (self.coords_in, self.tiles_in, *self.dense_in):
            copy.start()

    def greet(self):
        barrier = pltpu.get_barrier_semaphore()
        for device in self.friends():
            pl.semaphore_signal(barrier, inc=1, device_id=device, device_id_type=MESH)

    def friends(self):
        around = [self.neighbour(axis, step) for axis in range(2) for step in OTHERS]
        return [self.partner()] + [self.ring_device(step) for step in (1, -1, 2, -2)] + around

    def met(self):
        pl.semaphore_wait(pltpu.get_barrier_semaphore(), 11)

    def index_table(self):
        self.coords_in.wait()
        slot = lax.broadcasted_iota(jnp.int32, (SLOTS, SLOTS), 0)
        lane = lax.broadcasted_iota(jnp.int32, (SLOTS, SLOTS), 1)
        live = slot < self.count[0]
        lines = [None] * 8
        for column, prev, last in ((0, PREV_F, LAST_F), (1, PREV_B, LAST_B)):
            across = self.coords_v[column:column + 1, :]
            down = jnp.sum(jnp.where(slot == lane, across, 0), axis=1, keepdims=True)
            earlier = live & (slot < lane) & (down == across)
            lines[prev] = jnp.max(jnp.where(earlier, slot + 1, 0), axis=0, keepdims=True)
            lines[last] = jnp.max(jnp.where(live & (down == lane), slot + 1, 0), axis=0, keepdims=True)
            if column == 0:
                lines[ROW_ID] = across
            else:
                x, y, core, piece = across // 16, (across // 4) % 4, (across // 2) % 2, across % 2
                straight = piece == 0
                lines[PANEL_ID] = self.panel_at(piece, jnp.where(straight, x, y), jnp.where(straight, y, x), core)
        for at, line in enumerate(lines):
            self.table_v[at:at + 1, :] = jnp.zeros((1, SLOTS), jnp.int32) if line is None else line
        copy = pltpu.make_async_copy(self.table_v, self.table, self.in_sem.at[4])
        copy.start()
        for h in range(2):
            self.sums[h][0] = jnp.zeros((T, T), F32)
        copy.wait()

    def gather_across(self, h, piece, step1):
        first = self.along(piece, step1)
        at = self.panel_at(piece, first, self.at[1 - piece], self.core)
        tile = self.panel[h].at[at]
        for step in OTHERS:
            self.send(tile, tile, self.a_send.at[h], self.a2_sem.at[h, piece, step1 % SIDE], self.neighbour(1 - piece, step))

    def gather_own(self, h):
        self.landed(self.panel[h].at[pl.ds(0, 2)], self.own_sem.at[h])
        for piece in range(2):
            at = self.panel_at(piece, self.at[piece], self.at[1 - piece], self.core)
            tile = self.panel[h].at[at]
            for step in OTHERS:
                self.send(tile, tile, self.a_send.at[h], self.a1_sem.at[h, piece, step % SIDE - 1], self.neighbour(piece, step))
        for piece in range(2):
            self.gather_across(h, piece, 0)

    def gather_first(self, h):
        for step in (1, -1, 2):
            for piece in range(2):
                came = self.panel_at(piece, self.along(piece, -step), self.at[1 - piece], self.core)
                self.landed(self.panel[h].at[came], self.a1_sem.at[h, piece, step % SIDE - 1])
                self.gather_across(h, piece, -step)

    def gather_second(self, h):
        for step1 in (0, -1, 1, 2):
            for piece in range(2):
                first = self.panel_at(piece, self.along(piece, step1), 0, self.core)
                self.landed(self.panel[h].at[pl.ds(first, 3)], self.a2_sem.at[h, piece, step1 % SIDE])
                line = self.panel[h].at[pl.ds(first, SIDE)]
                self.send(line, line, self.a_send.at[h], self.ap_sem.at[h], self.partner())

    def gather_partner(self, h):
        self.landed(self.panel[h].at[pl.ds(0, 32)], self.ap_sem.at[h])

    def forward(self, h):
        sums, panel = self.sums[h], self.panel[h]

        def block(at, carry):
            for u in range(UNROLL):
                k = at * UNROLL + u
                product = jnp.dot(self.tiles[k], panel[self.table[PANEL_ID, k]], preferred_element_type=F32)
                sums[k + 1] = sums[self.table[PREV_F, k]] + product
            return carry

        lax.fori_loop(0, SLOTS // UNROLL, block, 0)

    def backward(self, h):
        sums, ga = self.sums[h], self.ga[h]

        def block(at, carry):
            for u in range(UNROLL):
                k = at * UNROLL + u
                product = jnp.dot(ga[self.table[ROW_ID, k]], self.tiles[k], preferred_element_type=F32)
                sums[k + 1] = sums[self.table[PREV_B, k]] + product
            return carry

        lax.fori_loop(0, SLOTS // UNROLL, block, 0)

    def row_sum(self, h, piece, step):
        return self.sums[h][self.table[LAST_F, self.ring(step) * 2 + piece]]

    def reduce_first(self, h, piece):
        for way in range(2):
            sign = 1 - 2 * way
            stage, middle = self.zs.at[h, piece, way], self.zm.at[h, piece, way]
            if way == piece:
                stage[1] = self.row_sum(h, piece, 4 * sign).astype(BF16)
                self.send(stage.at[1], middle.at[1], self.z_send.at[0], self.zm_sem.at[h, piece, way], self.ring_device(2 * sign))
            stage[0] = self.row_sum(h, piece, 3 * sign).astype(BF16)
            self.send(stage.at[0], middle.at[0], self.z_send.at[0], self.zm_sem.at[h, piece, way], self.ring_device(sign))
        for way in range(2):
            sign = 1 - 2 * way
            stage = self.zs.at[h, piece, way]
            stage[2] = self.row_sum(h, piece, sign).astype(BF16)
            self.send(stage.at[2], self.zr.at[h, piece, way], self.z_send.at[0], self.zr_sem.at[h, piece], self.ring_device(sign))

    def reduce_second(self, h, piece):
        for way in range(2):
            sign = 1 - 2 * way
            stage, middle = self.zs.at[h, piece, way], self.zm.at[h, piece, way]
            value = self.row_sum(h, piece, 2 * sign)
            if way == piece:
                self.landed(middle, self.zm_sem.at[h, piece, way])
                value = value + middle[0].astype(F32) + middle[1].astype(F32)
            else:
                self.landed(middle.at[0], self.zm_sem.at[h, piece, way])
                value = value + middle[0].astype(F32)
            stage[3] = value.astype(BF16)
            self.send(stage.at[3], self.zr.at[h, piece, 2 + way], self.z_send.at[0], self.zr_sem.at[h, piece], self.ring_device(2 * sign))

    def reduce_end(self, h, piece):
        self.landed(self.zr.at[h, piece], self.zr_sem.at[h, piece])
        value = self.row_sum(h, piece, 0)
        for came in range(4):
            value = value + self.zr[h, piece, came].astype(F32)
        self.agg[piece * T:(piece + 1) * T, h * T:(h + 1) * T] = value.astype(BF16)

    def dense(self, piece):
        rows = slice(piece * T, (piece + 1) * T)
        if piece == 0:
            for copy in self.dense_in:
                copy.wait()
        pre = jnp.dot(self.agg[rows, :], self.weight_v[...], preferred_element_type=F32)
        result, slope = gelu_pair(pre)
        grad_pre = (self.cot_v[rows, :].astype(F32) * slope).astype(BF16)
        turned = lax.dot_general(
            self.weight_v[...], grad_pre, (((1,), (1,)), ((), ())), preferred_element_type=F32).astype(BF16)
        for h in range(2):
            self.ga[h][self.z * 2 + piece] = turned[h * T:(h + 1) * T]
        self.hid_v[rows, :] = result.astype(BF16)
        self.grad_pre[rows, :] = grad_pre
        self.spread_own(0, piece)

    def weight_start(self):
        self.hidden_out = pltpu.make_async_copy(self.hid_v, self.hidden, self.out_sem.at[0])
        self.hidden_out.start()
        total = lax.dot_general(
            self.agg[...], self.grad_pre[...], (((0,), (0,)), ((), ())), preferred_element_type=F32)
        self.wg[...] = total.reshape(32, 8, 256)

        def start(step, carry):
            there = lax.rem(self.row + step, 32)
            self.send(self.wg.at[there], self.wg_row.at[self.row], self.w_sem.at[0], self.w_sem.at[1], (there, self.z))
            return carry

        lax.fori_loop(1, 32, start, 0)

    def weight_middle(self):
        self.landed(self.wg_row.at[pl.ds(0, 31)], self.w_sem.at[1])
        self.wg_row[self.row] = self.wg[self.row]
        part = jnp.sum(self.wg_row[...], axis=0)
        self.wg_part[...] = part
        self.wg_col[self.z] = part

        def start(step, carry):
            there = lax.rem(self.z + step, RING)
            self.send(self.wg_part, self.wg_col.at[self.z], self.w_sem.at[2], self.w_sem.at[3], (self.row, there))
            return carry

        lax.fori_loop(1, RING, start, 0)

    def weight_end(self):
        self.landed(self.wg_col.at[pl.ds(0, 7)], self.w_sem.at[3])
        self.wg_out[...] = jnp.sum(self.wg_col[...], axis=0)
        self.weight_out = pltpu.make_async_copy(self.wg_out, self.weight_grad, self.out_sem.at[1])
        self.weight_out.start()

    def spread(self, h, piece, source, step, sem):
        tile = self.ga[h].at[self.ring(source) * 2 + piece]
        self.send(tile, tile, self.d_send.at[0], sem, self.ring_device(step))

    def spread_own(self, h, piece):
        for way in range(2):
            self.spread(h, piece, 0, 2 - 4 * way, self.dm_sem.at[h, piece, way])
        for way in range(2):
            self.spread(h, piece, 0, 1 - 2 * way, self.dr_sem.at[h, piece])

    def spread_on(self, h, piece):
        for way in range(2):
            sign = 1 - 2 * way
            tile = self.ga[h].at[self.ring(-2 * sign) * 2 + piece]
            self.landed(tile, self.dm_sem.at[h, piece, way])
            if way == piece:
                self.spread(h, piece, -2 * sign, 2 * sign, self.dr_sem.at[h, piece])
            self.spread(h, piece, -2 * sign, sign, self.dr_sem.at[h, piece])

    def spread_end(self, h):
        for piece in range(2):
            self.landed(self.ga[h].at[pl.ds(0, 5)], self.dr_sem.at[h, piece])

    def grad_tile(self, h, piece, keep, step, core):
        reduce = self.along(1 - piece, step)
        x, y = (keep, reduce) if piece == 0 else (reduce, keep)
        return self.sums[h][self.table[LAST_B, ((x * SIDE + y) * 2 + core) * 2 + piece]]

    def grad_partner(self, h, line):
        keep = {piece: self.along(piece, LINES[line]) for piece in range(2)}
        for piece in range(2):
            for at, step in enumerate(LINES):
                self.ps[h, line, piece, at] = self.grad_tile(h, piece, keep[piece], step, 1 - self.core).astype(BF16)
        self.send(self.ps.at[h, line], self.pr.at[h, line], self.e_send.at[h], self.p_sem.at[h, line], self.partner())

    def chip_tile(self, h, line, piece, at):
        keep = self.along(piece, LINES[line])
        return self.grad_tile(h, piece, keep, LINES[at], self.core) + self.pr[h, line, piece, at].astype(F32)

    def grad_first(self, h, line):
        self.landed(self.pr.at[h, line], self.p_sem.at[h, line])
        for at, step in enumerate(OTHERS):
            for piece in range(2):
                self.s1[h, piece, line, at] = self.chip_tile(h, line, piece, at).astype(BF16)
                self.send(
                    self.s1.at[h, piece, line, at], self.r1.at[h, piece, line, at], self.e_send.at[h],
                    self.r1_sem.at[h, piece, line], self.neighbour(1 - piece, step))

    def grad_second(self, h, line):
        for piece in range(2):
            self.landed(self.r1.at[h, piece, line], self.r1_sem.at[h, piece, line])
            value = self.chip_tile(h, line, piece, 3)
            for at in range(3):
                value = value + self.r1[h, piece, line, at].astype(F32)
            if line == 3:
                self.axis_sum[h, piece] = value
                continue
            self.s2[h, piece, line] = value.astype(BF16)
            self.send(
                self.s2.at[h, piece, line], self.r2.at[h, piece, line], self.e_send.at[h],
                self.r2_sem.at[h, piece], self.neighbour(piece, LINES[line]))

    def grad_end(self, h):
        for piece in range(2):
            self.landed(self.r2.at[h, piece], self.r2_sem.at[h, piece])
            value = self.axis_sum[h, piece]
            for at in range(3):
                value = value + self.r2[h, piece, at].astype(F32)
            self.fg_v[piece * T:(piece + 1) * T, h * T:(h + 1) * T] = value.T

    def finish(self):
        out = pltpu.make_async_copy(self.fg_v, self.feature_grad, self.out_sem.at[2])
        out.start()
        self.drain()
        self.landed(self.wg_row.at[pl.ds(0, 31)], self.w_sem.at[0])
        self.landed(self.wg_col.at[pl.ds(0, 7)], self.w_sem.at[2])
        self.hidden_out.wait()
        self.weight_out.wait()
        out.wait()

    def drain(self, stages="azde"):
        some = self.panel0
        if "a" in stages:
            for h in range(2):
                self.landed(some.at[pl.ds(0, 62)], self.a_send.at[h])
        if "z" in stages:
            self.landed(some.at[pl.ds(0, 28)], self.z_send.at[0])
        if "d" in stages:
            self.landed(some.at[pl.ds(0, 28)], self.d_send.at[0])
        if "e" in stages:
            for h in range(2):
                self.landed(some.at[pl.ds(0, 62)], self.e_send.at[h])

    def run(self):
        self.greet()
        self.load()
        self.met()
        self.gather_own(0)
        self.gather_own(1)
        self.index_table()
        self.gather_first(0)
        self.gather_first(1)
        self.gather_second(0)
        self.gather_partner(0)
        self.tiles_in.wait()
        self.forward(0)
        for piece in range(2):
            self.reduce_first(0, piece)
        self.gather_second(1)
        for piece in range(2):
            self.reduce_second(0, piece)
        self.gather_partner(1)
        self.forward(1)
        for piece in range(2):
            self.reduce_first(1, piece)
        for piece in range(2):
            self.reduce_end(0, piece)
        for piece in range(2):
            self.reduce_second(1, piece)
        for piece in range(2):
            self.reduce_end(1, piece)
            self.dense(piece)
        for piece in range(2):
            self.spread_own(1, piece)
        self.weight_start()
        for h in range(2):
            for piece in range(2):
                self.spread_on(h, piece)
        self.spread_end(0)
        self.backward(0)
        for line in range(4):
            self.grad_partner(0, line)
        for line in range(4):
            self.grad_first(0, line)
        self.spread_end(1)
        self.backward(1)
        for line in range(4):
            self.grad_partner(1, line)
        for line in range(4):
            self.grad_second(0, line)
            self.grad_first(1, line)
        self.weight_middle()
        for line in range(4):
            self.grad_second(1, line)
        self.grad_end(0)
        self.weight_end()
        self.grad_end(1)
        self.finish()


def kernel(names, *refs):
    Layer(refs[:6], refs[6:9], dict(zip(names, refs[9:]))).run()


def hand_over(*refs):
    for source, target in zip(refs[:3], refs[3:]):
        target[...] = source[...]


def per_device(features, weight, tile_values, tile_coords, tile_count, cotangent):
    buffers = scratch()
    anywhere = pl.BlockSpec(memory_space=pl.ANY)
    shapes = (
        jax.ShapeDtypeStruct((256, 256), BF16),
        jax.ShapeDtypeStruct((8, 256), F32),
        jax.ShapeDtypeStruct((256, 256), F32),
    )
    results = pl.pallas_call(
        functools.partial(kernel, tuple(buffers)),
        out_shape=shapes,
        in_specs=[pl.BlockSpec(memory_space=pltpu.SMEM)] + [anywhere] * 5,
        out_specs=(anywhere, anywhere, anywhere),
        scratch_shapes=list(buffers.values()),
        compiler_params=pltpu.CompilerParams(
            collective_id=0, has_side_effects=True, vmem_limit_bytes=60 * 1024 * 1024),
        name="graph_layer",
    )(tile_count, features, weight, tile_values, tile_coords.T, cotangent)
    whole = pl.BlockSpec(memory_space=pltpu.VMEM)
    return pl.pallas_call(
        hand_over, out_shape=shapes, in_specs=[whole] * 3, out_specs=(whole, whole, whole), name="hand_over",
    )(*results)


def solution(mesh):
    return jax.shard_map(
        per_device,
        mesh=mesh,
        in_specs=(
            P(("row", "col"), None),
            P(),
            P(("row", "col"), None, None),
            P(("row", "col"), None),
            P(("row", "col")),
            P(("row", "col"), None),
        ),
        out_specs=(P(("row", "col"), None), P("row", None), P(("row", "col"), None)),
        check_vma=False,
    )
```

```python
import functools

import jax
import jax.numpy as jnp
from jax import lax
from jax.experimental import pallas as pl
from jax.experimental.pallas import tpu as pltpu
from jax.sharding import PartitionSpec as P

gelu_scale = 0.7978845608028654
gelu_cubic = 0.044715

MESH = pl.DeviceIdType.MESH
BF16 = jnp.bfloat16
F32 = jnp.float32
T = 128
SIDE = 4
RING = 8
SLOTS = 96
ROW_TILES = 16
COL_TILES = 64
UNROLL = 32

PREV_F, LAST_F, PREV_B, LAST_B, ROW_ID, PANEL_ID = range(6)

OTHERS = (2, 1, -1)
LINES = (2, 1, -1, 0)


def gelu_pair(values):
    inner = gelu_scale * (values + gelu_cubic * values * values * values)
    slope_tanh = jnp.tanh(inner)
    result = 0.5 * values * (1.0 + slope_tanh)
    slope = 0.5 * (1.0 + slope_tanh) + 0.5 * values * (
        1.0 - slope_tanh * slope_tanh
    ) * gelu_scale * (1.0 + 3.0 * gelu_cubic * values * values)
    return (result, slope)


def scratch():
    dma = pltpu.SemaphoreType.DMA
    return {
        "tiles": pltpu.VMEM((SLOTS, T, T), BF16),
        "weight_v": pltpu.VMEM((256, 256), BF16),
        "cot_v": pltpu.VMEM((256, 256), BF16),
        "coords_v": pltpu.VMEM((2, SLOTS), jnp.int32),
        "count_s": pltpu.SMEM((1,), jnp.int32),
        "table_v": pltpu.VMEM((8, SLOTS), jnp.int32),
        "table": pltpu.SMEM((8, SLOTS), jnp.int32),
        "panel0": pltpu.VMEM((COL_TILES, T, T), BF16),
        "panel1": pltpu.VMEM((COL_TILES, T, T), BF16),
        "sums0": pltpu.VMEM((SLOTS + 1, T, T), F32),
        "sums1": pltpu.VMEM((SLOTS + 1, T, T), F32),
        "zs": pltpu.VMEM((2, 2, 2, 4, T, T), BF16),
        "zm": pltpu.VMEM((2, 2, 2, 2, T, T), BF16),
        "zr": pltpu.VMEM((2, 2, 4, T, T), BF16),
        "agg": pltpu.VMEM((256, 256), BF16),
        "grad_pre": pltpu.VMEM((256, 256), BF16),
        "hid_v": pltpu.VMEM((256, 256), BF16),
        "wg": pltpu.VMEM((32, 8, 256), F32),
        "wg_row": pltpu.VMEM((32, 8, 256), F32),
        "wg_part": pltpu.VMEM((8, 256), F32),
        "wg_col": pltpu.VMEM((8, 8, 256), F32),
        "wg_out": pltpu.VMEM((8, 256), F32),
        "ga0": pltpu.VMEM((ROW_TILES, T, T), BF16),
        "ga1": pltpu.VMEM((ROW_TILES, T, T), BF16),
        "ps": pltpu.VMEM((2, SIDE, 2, SIDE, T, T), BF16),
        "pr": pltpu.VMEM((2, SIDE, 2, SIDE, T, T), BF16),
        "s1": pltpu.VMEM((2, 2, SIDE, 3, T, T), BF16),
        "r1": pltpu.VMEM((2, 2, SIDE, 3, T, T), BF16),
        "axis_sum": pltpu.VMEM((2, 2, T, T), F32),
        "s2": pltpu.VMEM((2, 2, 3, T, T), BF16),
        "r2": pltpu.VMEM((2, 2, 3, T, T), BF16),
        "fg_v": pltpu.VMEM((256, 256), F32),
        "own_sem": dma((2,)),
        "in_sem": dma((6,)),
        "out_sem": dma((3,)),
        "a_send": dma((2,)),
        "a1_sem": dma((2, 2, 3)),
        "a2_sem": dma((2, 2, 4)),
        "ap_sem": dma((2,)),
        "z_send": dma((1,)),
        "zm_sem": dma((2, 2, 2)),
        "zr_sem": dma((2, 2)),
        "d_send": dma((1,)),
        "dm_sem": dma((2, 2, 2)),
        "dr_sem": dma((2, 2)),
        "e_send": dma((2,)),
        "p_sem": dma((2, 4)),
        "r1_sem": dma((2, 2, SIDE)),
        "r2_sem": dma((2, 2)),
        "w_sem": dma((4,)),
    }


class Layer:
    def __init__(self, operands, results, refs):
        self.__dict__.update(refs)
        self.count, self.features, self.weight, self.tile_values, self.coords, self.cotangent = operands
        self.hidden, self.weight_grad, self.feature_grad = results
        self.panel = (self.panel0, self.panel1)
        self.sums = (self.sums0, self.sums1)
        self.ga = (self.ga0, self.ga1)
        self.row = lax.axis_index("row")
        self.z = lax.axis_index("col")
        self.core = lax.rem(self.row, 2)
        self.at = (self.row // 8, lax.rem(self.row // 2, SIDE))

    def along(self, axis, step):
        return lax.rem(self.at[axis] + step % SIDE, SIDE)

    def neighbour(self, axis, step):
        spot = [self.at[0], self.at[1]]
        spot[axis] = self.along(axis, step)
        return ((spot[0] * SIDE + spot[1]) * 2 + self.core, self.z)

    def partner(self):
        return (self.row + 1 - 2 * self.core, self.z)

    def ring(self, step):
        return lax.rem(self.z + step % RING, RING)

    def ring_device(self, step):
        return (self.row, self.ring(step))

    def panel_at(self, piece, first, second, core):
        return ((piece * 2 + core) * SIDE + first) * SIDE + second

    def send(self, src, dst, send_sem, recv_sem, device):
        pltpu.make_async_remote_copy(
            src_ref=src, dst_ref=dst, send_sem=send_sem, recv_sem=recv_sem,
            device_id=device, device_id_type=MESH,
        ).start()

    def landed(self, ref, sem):
        pltpu.make_async_copy(ref, ref, sem).wait()

    def load(self):
        self.own = []
        for h in range(2):
            for piece in range(2):
                at = self.panel_at(piece, self.at[piece], self.at[1 - piece], self.core)
                copy = pltpu.make_async_copy(
                    self.features.at[pl.ds(piece * T, T), pl.ds(h * T, T)], self.panel[h].at[at], self.own_sem.at[h])
                copy.start()
        sem = self.in_sem
        self.coords_in = pltpu.make_async_copy(self.coords, self.coords_v, sem.at[0])
        self.count_in = pltpu.make_async_copy(self.count, self.count_s, sem.at[5])
        self.tiles_in = pltpu.make_async_copy(self.tile_values, self.tiles, sem.at[1])
        self.dense_in = (
            pltpu.make_async_copy(self.weight, self.weight_v, sem.at[2]),
            pltpu.make_async_copy(self.cotangent, self.cot_v, sem.at[3]),
        )
        for copy in (self.coords_in, self.count_in, self.tiles_in, *self.dense_in):
            copy.start()

    def greet(self):
        barrier = pltpu.get_barrier_semaphore()
        for device in self.friends():
            pl.semaphore_signal(barrier, inc=1, device_id=device, device_id_type=MESH)

    def friends(self):
        around = [self.neighbour(axis, step) for axis in range(2) for step in OTHERS]
        return [self.partner()] + [self.ring_device(step) for step in (1, -1, 2, -2)] + around

    def met(self):
        pl.semaphore_wait(pltpu.get_barrier_semaphore(), 11)

    def index_table(self):
        self.coords_in.wait()
        self.count_in.wait()
        slot = lax.broadcasted_iota(jnp.int32, (SLOTS, SLOTS), 0)
        lane = lax.broadcasted_iota(jnp.int32, (SLOTS, SLOTS), 1)
        live = slot < self.count_s[0]
        lines = [None] * 8
        for column, prev, last in ((0, PREV_F, LAST_F), (1, PREV_B, LAST_B)):
            across = self.coords_v[column:column + 1, :]
            down = jnp.sum(jnp.where(slot == lane, across, 0), axis=1, keepdims=True)
            earlier = live & (slot < lane) & (down == across)
            lines[prev] = jnp.max(jnp.where(earlier, slot + 1, 0), axis=0, keepdims=True)
            lines[last] = jnp.max(jnp.where(live & (down == lane), slot + 1, 0), axis=0, keepdims=True)
            if column == 0:
                lines[ROW_ID] = across
            else:
                x, y, core, piece = across // 16, (across // 4) % 4, (across // 2) % 2, across % 2
                straight = piece == 0
                lines[PANEL_ID] = self.panel_at(piece, jnp.where(straight, x, y), jnp.where(straight, y, x), core)
        for at, line in enumerate(lines):
            self.table_v[at:at + 1, :] = jnp.zeros((1, SLOTS), jnp.int32) if line is None else line
        copy = pltpu.make_async_copy(self.table_v, self.table, self.in_sem.at[4])
        copy.start()
        for h in range(2):
            self.sums[h][0] = jnp.zeros((T, T), F32)
        copy.wait()

    def gather_across(self, h, piece, step1):
        first = self.along(piece, step1)
        at = self.panel_at(piece, first, self.at[1 - piece], self.core)
        tile = self.panel[h].at[at]
        for step in OTHERS:
            self.send(tile, tile, self.a_send.at[h], self.a2_sem.at[h, piece, step1 % SIDE], self.neighbour(1 - piece, step))

    def gather_own(self, h):
        self.landed(self.panel[h].at[pl.ds(0, 2)], self.own_sem.at[h])
        for piece in range(2):
            at = self.panel_at(piece, self.at[piece], self.at[1 - piece], self.core)
            tile = self.panel[h].at[at]
            for step in OTHERS:
                self.send(tile, tile, self.a_send.at[h], self.a1_sem.at[h, piece, step % SIDE - 1], self.neighbour(piece, step))

    def gather_first(self, h):
        for step in (1, -1, 2):
            for piece in range(2):
                came = self.panel_at(piece, self.along(piece, -step), self.at[1 - piece], self.core)
                self.landed(self.panel[h].at[came], self.a1_sem.at[h, piece, step % SIDE - 1])
                self.gather_across(h, piece, -step)

    def gather_second(self, h):
        for step1 in (0, -1, 1, 2):
            for piece in range(2):
                first = self.panel_at(piece, self.along(piece, step1), 0, self.core)
                self.landed(self.panel[h].at[pl.ds(first, 3)], self.a2_sem.at[h, piece, step1 % SIDE])
                line = self.panel[h].at[pl.ds(first, SIDE)]
                self.send(line, line, self.a_send.at[h], self.ap_sem.at[h], self.partner())

    def gather_partner(self, h):
        self.landed(self.panel[h].at[pl.ds(0, 32)], self.ap_sem.at[h])

    def forward(self, h):
        sums, panel = self.sums[h], self.panel[h]

        def block(at, carry):
            for u in range(UNROLL):
                k = at * UNROLL + u
                product = jnp.dot(self.tiles[k], panel[self.table[PANEL_ID, k]], preferred_element_type=F32)
                sums[k + 1] = sums[self.table[PREV_F, k]] + product
            return carry

        lax.fori_loop(0, SLOTS // UNROLL, block, 0)

    def backward(self, h):
        sums, ga = self.sums[h], self.ga[h]

        def block(at, carry):
            for u in range(UNROLL):
                k = at * UNROLL + u
                product = jnp.dot(ga[self.table[ROW_ID, k]], self.tiles[k], preferred_element_type=F32)
                sums[k + 1] = sums[self.table[PREV_B, k]] + product
            return carry

        lax.fori_loop(0, SLOTS // UNROLL, block, 0)

    def row_sum(self, h, piece, step):
        return self.sums[h][self.table[LAST_F, self.ring(step) * 2 + piece]]

    def reduce_first(self, h, piece):
        for way in range(2):
            sign = 1 - 2 * way
            stage, middle = self.zs.at[h, piece, way], self.zm.at[h, piece, way]
            if way == piece:
                stage[1] = self.row_sum(h, piece, 4 * sign).astype(BF16)
                self.send(stage.at[1], middle.at[1], self.z_send.at[0], self.zm_sem.at[h, piece, way], self.ring_device(2 * sign))
            stage[0] = self.row_sum(h, piece, 3 * sign).astype(BF16)
            self.send(stage.at[0], middle.at[0], self.z_send.at[0], self.zm_sem.at[h, piece, way], self.ring_device(sign))

    def reduce_near(self, h, piece):
        for way in range(2):
            sign = 1 - 2 * way
            stage = self.zs.at[h, piece, way]
            stage[2] = self.row_sum(h, piece, sign).astype(BF16)
            self.send(stage.at[2], self.zr.at[h, piece, way], self.z_send.at[0], self.zr_sem.at[h, piece], self.ring_device(sign))

    def reduce_second(self, h, piece):
        for way in range(2):
            sign = 1 - 2 * way
            stage, middle = self.zs.at[h, piece, way], self.zm.at[h, piece, way]
            value = self.row_sum(h, piece, 2 * sign)
            if way == piece:
                self.landed(middle, self.zm_sem.at[h, piece, way])
                value = value + middle[0].astype(F32) + middle[1].astype(F32)
            else:
                self.landed(middle.at[0], self.zm_sem.at[h, piece, way])
                value = value + middle[0].astype(F32)
            stage[3] = value.astype(BF16)
            self.send(stage.at[3], self.zr.at[h, piece, 2 + way], self.z_send.at[0], self.zr_sem.at[h, piece], self.ring_device(2 * sign))

    def reduce_end(self, h, piece):
        self.landed(self.zr.at[h, piece], self.zr_sem.at[h, piece])
        value = self.row_sum(h, piece, 0)
        for came in range(4):
            value = value + self.zr[h, piece, came].astype(F32)
        self.agg[piece * T:(piece + 1) * T, h * T:(h + 1) * T] = value.astype(BF16)

    def dense(self, piece):
        rows = slice(piece * T, (piece + 1) * T)
        if piece == 0:
            for copy in self.dense_in:
                copy.wait()
        pre = jnp.dot(self.agg[rows, :], self.weight_v[...], preferred_element_type=F32)
        result, slope = gelu_pair(pre)
        grad_pre = (self.cot_v[rows, :].astype(F32) * slope).astype(BF16)
        turned = lax.dot_general(
            self.weight_v[...], grad_pre, (((1,), (1,)), ((), ())), preferred_element_type=F32).astype(BF16)
        for h in range(2):
            self.ga[h][self.z * 2 + piece] = turned[h * T:(h + 1) * T]
        self.hid_v[rows, :] = result.astype(BF16)
        self.grad_pre[rows, :] = grad_pre
        self.spread_own(0, piece)

    def weight_start(self):
        self.hidden_out = pltpu.make_async_copy(self.hid_v, self.hidden, self.out_sem.at[0])
        self.hidden_out.start()
        total = lax.dot_general(
            self.agg[...], self.grad_pre[...], (((0,), (0,)), ((), ())), preferred_element_type=F32)
        self.wg[...] = total.reshape(32, 8, 256)

        def start(step, carry):
            there = lax.rem(self.row + step, 32)
            self.send(self.wg.at[there], self.wg_row.at[self.row], self.w_sem.at[0], self.w_sem.at[1], (there, self.z))
            return carry

        lax.fori_loop(1, 32, start, 0)

    def weight_middle(self):
        self.landed(self.wg_row.at[pl.ds(0, 31)], self.w_sem.at[1])
        self.wg_row[self.row] = self.wg[self.row]
        part = jnp.sum(self.wg_row[...], axis=0)
        self.wg_part[...] = part
        self.wg_col[self.z] = part

        def start(step, carry):
            there = lax.rem(self.z + step, RING)
            self.send(self.wg_part, self.wg_col.at[self.z], self.w_sem.at[2], self.w_sem.at[3], (self.row, there))
            return carry

        lax.fori_loop(1, RING, start, 0)

    def weight_end(self):
        self.landed(self.wg_col.at[pl.ds(0, 7)], self.w_sem.at[3])
        self.wg_out[...] = jnp.sum(self.wg_col[...], axis=0)
        self.weight_out = pltpu.make_async_copy(self.wg_out, self.weight_grad, self.out_sem.at[1])
        self.weight_out.start()

    def spread(self, h, piece, source, step, sem):
        tile = self.ga[h].at[self.ring(source) * 2 + piece]
        self.send(tile, tile, self.d_send.at[0], sem, self.ring_device(step))

    def spread_own(self, h, piece):
        for way in range(2):
            self.spread(h, piece, 0, 2 - 4 * way, self.dm_sem.at[h, piece, way])
        for way in range(2):
            self.spread(h, piece, 0, 1 - 2 * way, self.dr_sem.at[h, piece])

    def spread_on(self, h, piece):
        for way in range(2):
            sign = 1 - 2 * way
            tile = self.ga[h].at[self.ring(-2 * sign) * 2 + piece]
            self.landed(tile, self.dm_sem.at[h, piece, way])
            if way == piece:
                self.spread(h, piece, -2 * sign, 2 * sign, self.dr_sem.at[h, piece])
            self.spread(h, piece, -2 * sign, sign, self.dr_sem.at[h, piece])

    def spread_end(self, h):
        for piece in range(2):
            self.landed(self.ga[h].at[pl.ds(0, 5)], self.dr_sem.at[h, piece])

    def grad_tile(self, h, piece, keep, step, core):
        reduce = self.along(1 - piece, step)
        x, y = (keep, reduce) if piece == 0 else (reduce, keep)
        return self.sums[h][self.table[LAST_B, ((x * SIDE + y) * 2 + core) * 2 + piece]]

    def grad_partner(self, h, line):
        keep = {piece: self.along(piece, LINES[line]) for piece in range(2)}
        for piece in range(2):
            for at, step in enumerate(LINES):
                self.ps[h, line, piece, at] = self.grad_tile(h, piece, keep[piece], step, 1 - self.core).astype(BF16)
        self.send(self.ps.at[h, line], self.pr.at[h, line], self.e_send.at[h], self.p_sem.at[h, line], self.partner())

    def chip_tile(self, h, line, piece, at):
        keep = self.along(piece, LINES[line])
        return self.grad_tile(h, piece, keep, LINES[at], self.core) + self.pr[h, line, piece, at].astype(F32)

    def grad_first(self, h, line):
        self.landed(self.pr.at[h, line], self.p_sem.at[h, line])
        for at, step in enumerate(OTHERS):
            for piece in range(2):
                self.s1[h, piece, line, at] = self.chip_tile(h, line, piece, at).astype(BF16)
                self.send(
                    self.s1.at[h, piece, line, at], self.r1.at[h, piece, line, at], self.e_send.at[h],
                    self.r1_sem.at[h, piece, line], self.neighbour(1 - piece, step))

    def grad_second(self, h, line):
        for piece in range(2):
            self.landed(self.r1.at[h, piece, line], self.r1_sem.at[h, piece, line])
            value = self.chip_tile(h, line, piece, 3)
            for at in range(3):
                value = value + self.r1[h, piece, line, at].astype(F32)
            if line == 3:
                self.axis_sum[h, piece] = value
                continue
            self.s2[h, piece, line] = value.astype(BF16)
            self.send(
                self.s2.at[h, piece, line], self.r2.at[h, piece, line], self.e_send.at[h],
                self.r2_sem.at[h, piece], self.neighbour(piece, LINES[line]))

    def grad_end(self, h):
        for piece in range(2):
            self.landed(self.r2.at[h, piece], self.r2_sem.at[h, piece])
            value = self.axis_sum[h, piece]
            for at in range(3):
                value = value + self.r2[h, piece, at].astype(F32)
            self.fg_v[piece * T:(piece + 1) * T, h * T:(h + 1) * T] = value.T

    def finish(self):
        out = pltpu.make_async_copy(self.fg_v, self.feature_grad, self.out_sem.at[2])
        out.start()
        self.drain()
        self.landed(self.wg_row.at[pl.ds(0, 31)], self.w_sem.at[0])
        self.landed(self.wg_col.at[pl.ds(0, 7)], self.w_sem.at[2])
        self.hidden_out.wait()
        self.weight_out.wait()
        out.wait()

    def drain(self, stages="azde"):
        some = self.panel0
        if "a" in stages:
            for h in range(2):
                self.landed(some.at[pl.ds(0, 62)], self.a_send.at[h])
        if "z" in stages:
            self.landed(some.at[pl.ds(0, 28)], self.z_send.at[0])
        if "d" in stages:
            self.landed(some.at[pl.ds(0, 28)], self.d_send.at[0])
        if "e" in stages:
            for h in range(2):
                self.landed(some.at[pl.ds(0, 62)], self.e_send.at[h])

    def run(self):
        self.greet()
        self.load()
        self.met()
        self.gather_own(0)
        for piece in range(2):
            self.gather_across(0, piece, 0)
        self.gather_own(1)
        self.index_table()
        self.gather_first(0)
        for piece in range(2):
            self.gather_across(1, piece, 0)
        self.gather_first(1)
        self.gather_second(0)
        self.gather_partner(0)
        self.tiles_in.wait()
        self.forward(0)
        for piece in range(2):
            self.reduce_first(0, piece)
        for piece in range(2):
            self.reduce_near(0, piece)
        self.gather_second(1)
        for piece in range(2):
            self.reduce_second(0, piece)
        self.gather_partner(1)
        self.forward(1)
        for piece in range(2):
            self.reduce_first(1, piece)
        for piece in range(2):
            self.reduce_near(1, piece)
        for piece in range(2):
            self.reduce_end(0, piece)
        for piece in range(2):
            self.reduce_second(1, piece)
        for piece in range(2):
            self.reduce_end(1, piece)
            self.dense(piece)
        for piece in range(2):
            self.spread_on(0, piece)
        for piece in range(2):
            self.spread_own(1, piece)
        self.weight_start()
        for piece in range(2):
            self.spread_on(1, piece)
        self.spread_end(0)
        self.backward(0)
        for line in range(4):
            self.grad_partner(0, line)
        for line in range(4):
            self.grad_first(0, line)
        self.spread_end(1)
        self.backward(1)
        for line in range(4):
            self.grad_partner(1, line)
        for line in range(4):
            self.grad_second(0, line)
            self.grad_first(1, line)
        self.weight_middle()
        for line in range(4):
            self.grad_second(1, line)
        self.grad_end(0)
        self.weight_end()
        self.grad_end(1)
        self.finish()


def kernel(names, *refs):
    Layer(refs[:6], refs[6:9], dict(zip(names, refs[9:]))).run()


def hand_over(*refs):
    for source, target in zip(refs[:3], refs[3:]):
        target[...] = source[...]


def per_device(features, weight, tile_values, tile_coords, tile_count, cotangent):
    buffers = scratch()
    anywhere = pl.BlockSpec(memory_space=pl.ANY)
    shapes = (
        jax.ShapeDtypeStruct((256, 256), BF16),
        jax.ShapeDtypeStruct((8, 256), F32),
        jax.ShapeDtypeStruct((256, 256), F32),
    )
    results = pl.pallas_call(
        functools.partial(kernel, tuple(buffers)),
        out_shape=shapes,
        in_specs=[anywhere] * 6,
        out_specs=(anywhere, anywhere, anywhere),
        scratch_shapes=list(buffers.values()),
        compiler_params=pltpu.CompilerParams(
            collective_id=0, has_side_effects=True, vmem_limit_bytes=60 * 1024 * 1024),
        name="graph_layer",
    )(tile_count, features, weight, tile_values, tile_coords.T, cotangent)
    whole = pl.BlockSpec(memory_space=pltpu.VMEM)
    return pl.pallas_call(
        hand_over, out_shape=shapes, in_specs=[whole] * 3, out_specs=(whole, whole, whole), name="hand_over",
    )(*results)


def solution(mesh):
    return jax.shard_map(
        per_device,
        mesh=mesh,
        in_specs=(
            P(("row", "col"), None),
            P(),
            P(("row", "col"), None, None),
            P(("row", "col"), None),
            P(("row", "col")),
            P(("row", "col"), None),
        ),
        out_specs=(P(("row", "col"), None), P("row", None), P(("row", "col"), None)),
        check_vma=False,
    )
```

```python
import functools

import jax
import jax.numpy as jnp
from jax import lax
from jax.experimental import pallas as pl
from jax.experimental.pallas import tpu as pltpu
from jax.sharding import PartitionSpec as P

gelu_scale = 0.7978845608028654
gelu_cubic = 0.044715

MESH = pl.DeviceIdType.MESH
BF16 = jnp.bfloat16
F32 = jnp.float32
T = 128
SIDE = 4
RING = 8
SLOTS = 96
ROW_TILES = 16
COL_TILES = 64
UNROLL = 32

PREV_F, LAST_F, PREV_B, LAST_B, ROW_ID, PANEL_ID = range(6)

OTHERS = (2, 1, -1)
LINES = (2, 1, -1, 0)


def gelu_pair(values):
    inner = gelu_scale * (values + gelu_cubic * values * values * values)
    slope_tanh = jnp.tanh(inner)
    result = 0.5 * values * (1.0 + slope_tanh)
    slope = 0.5 * (1.0 + slope_tanh) + 0.5 * values * (
        1.0 - slope_tanh * slope_tanh
    ) * gelu_scale * (1.0 + 3.0 * gelu_cubic * values * values)
    return (result, slope)


def scratch():
    dma = pltpu.SemaphoreType.DMA
    return {
        "tiles": pltpu.VMEM((SLOTS, T, T), BF16),
        "weight_v": pltpu.VMEM((256, 256), BF16),
        "cot_v": pltpu.VMEM((256, 256), BF16),
        "coords_v": pltpu.VMEM((2, SLOTS), jnp.int32),
        "count_s": pltpu.SMEM((1,), jnp.int32),
        "table_v": pltpu.VMEM((8, SLOTS), jnp.int32),
        "table": pltpu.SMEM((8, SLOTS), jnp.int32),
        "panel0": pltpu.VMEM((COL_TILES, T, T), BF16),
        "panel1": pltpu.VMEM((COL_TILES, T, T), BF16),
        "sums0": pltpu.VMEM((SLOTS + 1, T, T), F32),
        "sums1": pltpu.VMEM((SLOTS + 1, T, T), F32),
        "zs": pltpu.VMEM((2, 2, 2, 4, T, T), BF16),
        "zm": pltpu.VMEM((2, 2, 2, 2, T, T), BF16),
        "zr": pltpu.VMEM((2, 2, 4, T, T), BF16),
        "agg": pltpu.VMEM((256, 256), BF16),
        "grad_pre": pltpu.VMEM((256, 256), BF16),
        "hid_v": pltpu.VMEM((256, 256), BF16),
        "wg": pltpu.VMEM((32, 8, 256), F32),
        "wg_row": pltpu.VMEM((32, 8, 256), F32),
        "wg_part": pltpu.VMEM((8, 256), F32),
        "wg_col": pltpu.VMEM((8, 8, 256), F32),
        "wg_out": pltpu.VMEM((8, 256), F32),
        "ga0": pltpu.VMEM((ROW_TILES, T, T), BF16),
        "ga1": pltpu.VMEM((ROW_TILES, T, T), BF16),
        "ps": pltpu.VMEM((2, SIDE, 2, SIDE, T, T), BF16),
        "pr": pltpu.VMEM((2, SIDE, 2, SIDE, T, T), BF16),
        "s1": pltpu.VMEM((2, 2, SIDE, 3, T, T), BF16),
        "r1": pltpu.VMEM((2, 2, SIDE, 3, T, T), BF16),
        "rf": pltpu.VMEM((2, 2, 2, T, T), BF16),
        "axis_sum": pltpu.VMEM((2, 2, T, T), F32),
        "s2": pltpu.VMEM((2, 2, 3, T, T), BF16),
        "r2": pltpu.VMEM((2, 2, 4, T, T), BF16),
        "fg_v": pltpu.VMEM((256, 256), F32),
        "own_sem": dma((2,)),
        "in_sem": dma((6,)),
        "out_sem": dma((4,)),
        "a_send": dma((2,)),
        "a1_sem": dma((2, 2, 3)),
        "a2_sem": dma((2, 2, 4)),
        "a3_sem": dma((2, 2)),
        "ap_sem": dma((2,)),
        "z_send": dma((1,)),
        "zm_sem": dma((2, 2, 2)),
        "zr_sem": dma((2, 2)),
        "d_send": dma((1,)),
        "dm_sem": dma((2, 2, 2)),
        "dr_sem": dma((2, 2)),
        "e_send": dma((2,)),
        "p_sem": dma((2, 4)),
        "r1_sem": dma((2, 2, SIDE)),
        "rf_sem": dma((2, 2)),
        "r2_sem": dma((2, 2)),
        "w_sem": dma((4,)),
    }


class Layer:
    def __init__(self, operands, results, refs):
        self.__dict__.update(refs)
        self.count, self.features, self.weight, self.tile_values, self.coords, self.cotangent = operands
        self.hidden, self.weight_grad, self.feature_grad = results
        self.panel = (self.panel0, self.panel1)
        self.sums = (self.sums0, self.sums1)
        self.ga = (self.ga0, self.ga1)
        self.row = lax.axis_index("row")
        self.z = lax.axis_index("col")
        self.core = lax.rem(self.row, 2)
        self.at = (self.row // 8, lax.rem(self.row // 2, SIDE))

    def along(self, axis, step):
        return lax.rem(self.at[axis] + step % SIDE, SIDE)

    def neighbour(self, axis, step):
        spot = [self.at[0], self.at[1]]
        spot[axis] = self.along(axis, step)
        return ((spot[0] * SIDE + spot[1]) * 2 + self.core, self.z)

    def partner(self):
        return (self.row + 1 - 2 * self.core, self.z)

    def ring(self, step):
        return lax.rem(self.z + step % RING, RING)

    def ring_device(self, step):
        return (self.row, self.ring(step))

    def panel_at(self, piece, first, second, core):
        return ((piece * 2 + core) * SIDE + first) * SIDE + second

    def send(self, src, dst, send_sem, recv_sem, device):
        pltpu.make_async_remote_copy(
            src_ref=src, dst_ref=dst, send_sem=send_sem, recv_sem=recv_sem,
            device_id=device, device_id_type=MESH,
        ).start()

    def landed(self, ref, sem):
        pltpu.make_async_copy(ref, ref, sem).wait()

    def load(self):
        self.grads_out = []
        for h in range(2):
            for piece in range(2):
                at = self.panel_at(piece, self.at[piece], self.at[1 - piece], self.core)
                copy = pltpu.make_async_copy(
                    self.features.at[pl.ds(piece * T, T), pl.ds(h * T, T)], self.panel[h].at[at], self.own_sem.at[h])
                copy.start()
        sem = self.in_sem
        self.coords_in = pltpu.make_async_copy(self.coords, self.coords_v, sem.at[0])
        self.count_in = pltpu.make_async_copy(self.count, self.count_s, sem.at[5])
        self.tiles_in = pltpu.make_async_copy(self.tile_values, self.tiles, sem.at[1])
        self.dense_in = (
            pltpu.make_async_copy(self.weight, self.weight_v, sem.at[2]),
            pltpu.make_async_copy(self.cotangent, self.cot_v, sem.at[3]),
        )
        for copy in (self.coords_in, self.count_in, self.tiles_in, *self.dense_in):
            copy.start()

    def greet(self):
        barrier = pltpu.get_barrier_semaphore()
        for device in self.friends():
            pl.semaphore_signal(barrier, inc=1, device_id=device, device_id_type=MESH)

    def friends(self):
        around = [self.neighbour(axis, step) for axis in range(2) for step in OTHERS]
        return [self.partner()] + [self.ring_device(step) for step in (1, -1, 2, -2)] + around

    def met(self):
        pl.semaphore_wait(pltpu.get_barrier_semaphore(), 11)

    def index_table(self):
        self.coords_in.wait()
        self.count_in.wait()
        slot = lax.broadcasted_iota(jnp.int32, (SLOTS, SLOTS), 0)
        lane = lax.broadcasted_iota(jnp.int32, (SLOTS, SLOTS), 1)
        live = slot < self.count_s[0]
        lines = [None] * 8
        for column, prev, last in ((0, PREV_F, LAST_F), (1, PREV_B, LAST_B)):
            across = self.coords_v[column:column + 1, :]
            down = jnp.sum(jnp.where(slot == lane, across, 0), axis=1, keepdims=True)
            earlier = live & (slot < lane) & (down == across)
            lines[prev] = jnp.max(jnp.where(earlier, slot + 1, 0), axis=0, keepdims=True)
            lines[last] = jnp.max(jnp.where(live & (down == lane), slot + 1, 0), axis=0, keepdims=True)
            if column == 0:
                lines[ROW_ID] = across
            else:
                x, y, core, piece = across // 16, (across // 4) % 4, (across // 2) % 2, across % 2
                straight = piece == 0
                lines[PANEL_ID] = self.panel_at(piece, jnp.where(straight, x, y), jnp.where(straight, y, x), core)
        for at, line in enumerate(lines):
            self.table_v[at:at + 1, :] = jnp.zeros((1, SLOTS), jnp.int32) if line is None else line
        copy = pltpu.make_async_copy(self.table_v, self.table, self.in_sem.at[4])
        copy.start()
        for h in range(2):
            self.sums[h][0] = jnp.zeros((T, T), F32)
        copy.wait()

    def gather_across(self, h, piece, step1):
        first = self.along(piece, step1)
        tile = self.panel[h].at[self.panel_at(piece, first, self.at[1 - piece], self.core)]
        for step in OTHERS:
            if step == 2 and step1 in (1, -1):
                continue
            sem = self.a3_sem.at[h, piece] if step == 2 and step1 == 0 else self.a2_sem.at[h, piece, step1 % SIDE]
            self.send(tile, tile, self.a_send.at[h], sem, self.neighbour(1 - piece, step))

    def gather_far(self, h):
        for piece in range(2):
            at = self.panel_at(piece, self.at[piece], self.along(1 - piece, 2), self.core)
            tile = self.panel[h].at[at]
            self.landed(tile, self.a3_sem.at[h, piece])
            for step in (1, -1):
                self.send(tile, tile, self.a_send.at[h], self.a2_sem.at[h, piece, -step % SIDE], self.neighbour(piece, step))

    def gather_own(self, h):
        self.landed(self.panel[h].at[pl.ds(0, 2)], self.own_sem.at[h])
        for piece in range(2):
            at = self.panel_at(piece, self.at[piece], self.at[1 - piece], self.core)
            tile = self.panel[h].at[at]
            for step in OTHERS:
                self.send(tile, tile, self.a_send.at[h], self.a1_sem.at[h, piece, step % SIDE - 1], self.neighbour(piece, step))

    def gather_first(self, h):
        for step in (1, -1, 2):
            for piece in range(2):
                came = self.panel_at(piece, self.along(piece, -step), self.at[1 - piece], self.core)
                self.landed(self.panel[h].at[came], self.a1_sem.at[h, piece, step % SIDE - 1])
                self.gather_across(h, piece, -step)

    def gather_second(self, h):
        for step1 in (0, -1, 1, 2):
            for piece in range(2):
                first = self.panel_at(piece, self.along(piece, step1), 0, self.core)
                self.landed(self.panel[h].at[pl.ds(first, 2 if step1 == 0 else 3)], self.a2_sem.at[h, piece, step1 % SIDE])
                line = self.panel[h].at[pl.ds(first, SIDE)]
                self.send(line, line, self.a_send.at[h], self.ap_sem.at[h], self.partner())

    def gather_partner(self, h):
        self.landed(self.panel[h].at[pl.ds(0, 32)], self.ap_sem.at[h])

    def forward(self, h):
        sums, panel = self.sums[h], self.panel[h]

        def block(at, carry):
            for u in range(UNROLL):
                k = at * UNROLL + u
                product = jnp.dot(self.tiles[k], panel[self.table[PANEL_ID, k]], preferred_element_type=F32)
                sums[k + 1] = sums[self.table[PREV_F, k]] + product
            return carry

        lax.fori_loop(0, SLOTS // UNROLL, block, 0)

    def backward(self, h):
        sums, ga = self.sums[h], self.ga[h]

        def block(at, carry):
            for u in range(UNROLL):
                k = at * UNROLL + u
                product = jnp.dot(ga[self.table[ROW_ID, k]], self.tiles[k], preferred_element_type=F32)
                sums[k + 1] = sums[self.table[PREV_B, k]] + product
            return carry

        lax.fori_loop(0, SLOTS // UNROLL, block, 0)

    def row_sum(self, h, piece, step):
        return self.sums[h][self.table[LAST_F, self.ring(step) * 2 + piece]]

    def reduce_first(self, h, piece):
        for way in range(2):
            sign = 1 - 2 * way
            stage, middle = self.zs.at[h, piece, way], self.zm.at[h, piece, way]
            if way == piece:
                stage[1] = self.row_sum(h, piece, 4 * sign).astype(BF16)
                self.send(stage.at[1], middle.at[1], self.z_send.at[0], self.zm_sem.at[h, piece, way], self.ring_device(2 * sign))
            stage[0] = self.row_sum(h, piece, 3 * sign).astype(BF16)
            self.send(stage.at[0], middle.at[0], self.z_send.at[0], self.zm_sem.at[h, piece, way], self.ring_device(sign))

    def reduce_near(self, h, piece):
        for way in range(2):
            sign = 1 - 2 * way
            stage = self.zs.at[h, piece, way]
            stage[2] = self.row_sum(h, piece, sign).astype(BF16)
            self.send(stage.at[2], self.zr.at[h, piece, way], self.z_send.at[0], self.zr_sem.at[h, piece], self.ring_device(sign))

    def reduce_second(self, h, piece):
        for way in range(2):
            sign = 1 - 2 * way
            stage, middle = self.zs.at[h, piece, way], self.zm.at[h, piece, way]
            value = self.row_sum(h, piece, 2 * sign)
            if way == piece:
                self.landed(middle, self.zm_sem.at[h, piece, way])
                value = value + middle[0].astype(F32) + middle[1].astype(F32)
            else:
                self.landed(middle.at[0], self.zm_sem.at[h, piece, way])
                value = value + middle[0].astype(F32)
            stage[3] = value.astype(BF16)
            self.send(stage.at[3], self.zr.at[h, piece, 2 + way], self.z_send.at[0], self.zr_sem.at[h, piece], self.ring_device(2 * sign))

    def reduce_end(self, h, piece):
        self.landed(self.zr.at[h, piece], self.zr_sem.at[h, piece])
        value = self.row_sum(h, piece, 0)
        for came in range(4):
            value = value + self.zr[h, piece, came].astype(F32)
        self.agg[piece * T:(piece + 1) * T, h * T:(h + 1) * T] = value.astype(BF16)

    def dense(self, piece):
        rows = slice(piece * T, (piece + 1) * T)
        if piece == 0:
            for copy in self.dense_in:
                copy.wait()
        pre = jnp.dot(self.agg[rows, :], self.weight_v[...], preferred_element_type=F32)
        result, slope = gelu_pair(pre)
        grad_pre = (self.cot_v[rows, :].astype(F32) * slope).astype(BF16)
        turned = lax.dot_general(
            self.weight_v[...], grad_pre, (((1,), (1,)), ((), ())), preferred_element_type=F32).astype(BF16)
        for h in range(2):
            self.ga[h][self.z * 2 + piece] = turned[h * T:(h + 1) * T]
        self.hid_v[rows, :] = result.astype(BF16)
        self.grad_pre[rows, :] = grad_pre
        self.spread_own(0, piece)

    def weight_start(self):
        self.hidden_out = pltpu.make_async_copy(self.hid_v, self.hidden, self.out_sem.at[0])
        self.hidden_out.start()
        total = lax.dot_general(
            self.agg[...], self.grad_pre[...], (((0,), (0,)), ((), ())), preferred_element_type=F32)
        self.wg[...] = total.reshape(32, 8, 256)

        def start(step, carry):
            there = lax.rem(self.row + step, 32)
            self.send(self.wg.at[there], self.wg_row.at[self.row], self.w_sem.at[0], self.w_sem.at[1], (there, self.z))
            return carry

        lax.fori_loop(1, 32, start, 0)

    def weight_middle(self):
        self.landed(self.wg_row.at[pl.ds(0, 31)], self.w_sem.at[1])
        self.wg_row[self.row] = self.wg[self.row]
        part = jnp.sum(self.wg_row[...], axis=0)
        self.wg_part[...] = part
        self.wg_col[self.z] = part

        def start(step, carry):
            there = lax.rem(self.z + step, RING)
            self.send(self.wg_part, self.wg_col.at[self.z], self.w_sem.at[2], self.w_sem.at[3], (self.row, there))
            return carry

        lax.fori_loop(1, RING, start, 0)

    def weight_end(self):
        self.landed(self.wg_col.at[pl.ds(0, 7)], self.w_sem.at[3])
        self.wg_out[...] = jnp.sum(self.wg_col[...], axis=0)
        self.weight_out = pltpu.make_async_copy(self.wg_out, self.weight_grad, self.out_sem.at[1])
        self.weight_out.start()

    def spread(self, h, piece, source, step, sem):
        tile = self.ga[h].at[self.ring(source) * 2 + piece]
        self.send(tile, tile, self.d_send.at[0], sem, self.ring_device(step))

    def spread_own(self, h, piece):
        for way in range(2):
            self.spread(h, piece, 0, 2 - 4 * way, self.dm_sem.at[h, piece, way])
        for way in range(2):
            self.spread(h, piece, 0, 1 - 2 * way, self.dr_sem.at[h, piece])

    def spread_on(self, h, piece):
        for way in range(2):
            sign = 1 - 2 * way
            tile = self.ga[h].at[self.ring(-2 * sign) * 2 + piece]
            self.landed(tile, self.dm_sem.at[h, piece, way])
            if way == piece:
                self.spread(h, piece, -2 * sign, 2 * sign, self.dr_sem.at[h, piece])
            self.spread(h, piece, -2 * sign, sign, self.dr_sem.at[h, piece])

    def spread_end(self, h):
        for piece in range(2):
            self.landed(self.ga[h].at[pl.ds(0, 5)], self.dr_sem.at[h, piece])

    def grad_tile(self, h, piece, keep, step, core):
        reduce = self.along(1 - piece, step)
        x, y = (keep, reduce) if piece == 0 else (reduce, keep)
        return self.sums[h][self.table[LAST_B, ((x * SIDE + y) * 2 + core) * 2 + piece]]

    def grad_partner(self, h, line):
        keep = {piece: self.along(piece, LINES[line]) for piece in range(2)}
        for piece in range(2):
            for at, step in enumerate(LINES):
                self.ps[h, line, piece, at] = self.grad_tile(h, piece, keep[piece], step, 1 - self.core).astype(BF16)
        self.send(self.ps.at[h, line], self.pr.at[h, line], self.e_send.at[h], self.p_sem.at[h, line], self.partner())

    def chip_tile(self, h, line, piece, at):
        keep = self.along(piece, LINES[line])
        return self.grad_tile(h, piece, keep, LINES[at], self.core) + self.pr[h, line, piece, at].astype(F32)

    def grad_first(self, h, line):
        self.landed(self.pr.at[h, line], self.p_sem.at[h, line])
        for at, step in enumerate(OTHERS):
            if at == 0 and line == 3:
                continue
            for piece in range(2):
                self.s1[h, piece, line, at] = self.chip_tile(h, line, piece, at).astype(BF16)
                if at == 0 and line in (1, 2):
                    target, sem, device = self.rf.at[h, piece, line - 1], self.rf_sem.at[h, piece], self.neighbour(piece, LINES[line])
                else:
                    target, sem = self.r1.at[h, piece, line, at], self.r1_sem.at[h, piece, line]
                    device = self.neighbour(1 - piece, step)
                self.send(self.s1.at[h, piece, line, at], target, self.e_send.at[h], sem, device)

    def grad_far(self, h):
        for piece in range(2):
            self.landed(self.rf.at[h, piece], self.rf_sem.at[h, piece])
            value = self.chip_tile(h, 3, piece, 0) + self.rf[h, piece, 0].astype(F32) + self.rf[h, piece, 1].astype(F32)
            self.s1[h, piece, 3, 0] = value.astype(BF16)
            self.send(
                self.s1.at[h, piece, 3, 0], self.r2.at[h, piece, 3], self.e_send.at[h],
                self.r2_sem.at[h, piece], self.neighbour(1 - piece, 2))

    def grad_second(self, h, line):
        far = 0 if line == 0 else 1
        for piece in range(2):
            self.landed(self.r1.at[h, piece, line, pl.ds(far, 3 - far)], self.r1_sem.at[h, piece, line])
            value = self.chip_tile(h, line, piece, 3)
            for at in range(far, 3):
                value = value + self.r1[h, piece, line, at].astype(F32)
            if line == 3:
                self.axis_sum[h, piece] = value
                continue
            self.s2[h, piece, line] = value.astype(BF16)
            self.send(
                self.s2.at[h, piece, line], self.r2.at[h, piece, line], self.e_send.at[h],
                self.r2_sem.at[h, piece], self.neighbour(piece, LINES[line]))

    def grad_end(self, h):
        for piece in range(2):
            self.landed(self.r2.at[h, piece], self.r2_sem.at[h, piece])
            value = self.axis_sum[h, piece]
            for at in range(4):
                value = value + self.r2[h, piece, at].astype(F32)
            self.fg_v[piece * T:(piece + 1) * T, h * T:(h + 1) * T] = value.T
        columns = pl.ds(h * T, T)
        out = pltpu.make_async_copy(self.fg_v.at[:, columns], self.feature_grad.at[:, columns], self.out_sem.at[2 + h])
        out.start()
        self.grads_out.append(out)

    def finish(self):
        self.drain()
        self.landed(self.wg_row.at[pl.ds(0, 31)], self.w_sem.at[0])
        self.landed(self.wg_col.at[pl.ds(0, 7)], self.w_sem.at[2])
        self.hidden_out.wait()
        self.weight_out.wait()
        for out in self.grads_out:
            out.wait()

    def drain(self, stages="azde"):
        some = self.panel0
        if "a" in stages:
            for h in range(2):
                self.landed(some.at[pl.ds(0, 62)], self.a_send.at[h])
        if "z" in stages:
            self.landed(some.at[pl.ds(0, 28)], self.z_send.at[0])
        if "d" in stages:
            self.landed(some.at[pl.ds(0, 28)], self.d_send.at[0])
        if "e" in stages:
            for h in range(2):
                self.landed(some.at[pl.ds(0, 62)], self.e_send.at[h])

    def run(self):
        self.greet()
        self.load()
        self.met()
        self.gather_own(0)
        for piece in range(2):
            self.gather_across(0, piece, 0)
        self.gather_own(1)
        self.index_table()
        self.gather_first(0)
        self.gather_far(0)
        for piece in range(2):
            self.gather_across(1, piece, 0)
        self.gather_first(1)
        self.gather_far(1)
        self.gather_second(0)
        self.gather_partner(0)
        self.tiles_in.wait()
        self.forward(0)
        for piece in range(2):
            self.reduce_first(0, piece)
        for piece in range(2):
            self.reduce_near(0, piece)
        self.gather_second(1)
        for piece in range(2):
            self.reduce_second(0, piece)
        self.gather_partner(1)
        self.forward(1)
        for piece in range(2):
            self.reduce_first(1, piece)
        for piece in range(2):
            self.reduce_near(1, piece)
        for piece in range(2):
            self.reduce_end(0, piece)
        for piece in range(2):
            self.reduce_second(1, piece)
        for piece in range(2):
            self.reduce_end(1, piece)
            self.dense(piece)
        for piece in range(2):
            self.spread_on(0, piece)
        for piece in range(2):
            self.spread_own(1, piece)
        self.weight_start()
        for piece in range(2):
            self.spread_on(1, piece)
        self.spread_end(0)
        self.backward(0)
        for line in range(4):
            self.grad_partner(0, line)
        for line in range(4):
            self.grad_first(0, line)
        self.spread_end(1)
        self.backward(1)
        for line in range(4):
            self.grad_partner(1, line)
        for line in range(4):
            self.grad_second(0, line)
            if line == 2:
                self.grad_far(0)
            self.grad_first(1, line)
        self.weight_middle()
        for line in range(4):
            self.grad_second(1, line)
            if line == 2:
                self.grad_far(1)
        self.grad_end(0)
        self.weight_end()
        self.grad_end(1)
        self.finish()


def kernel(names, *refs):
    Layer(refs[:6], refs[6:9], dict(zip(names, refs[9:]))).run()


def hand_over(*refs):
    sources, targets, middle, sem = refs[:3], refs[3:6], refs[6:9], refs[9]
    inward = [pltpu.make_async_copy(a, b, sem.at[i]) for i, (a, b) in enumerate(zip(sources, middle))]
    outward = [pltpu.make_async_copy(a, b, sem.at[3 + i]) for i, (a, b) in enumerate(zip(middle, targets))]
    for copy in inward:
        copy.start()
    for came, leaves in zip(inward, outward):
        came.wait()
        leaves.start()
    for copy in outward:
        copy.wait()


def per_device(features, weight, tile_values, tile_coords, tile_count, cotangent):
    buffers = scratch()
    anywhere = pl.BlockSpec(memory_space=pl.ANY)
    shapes = (
        jax.ShapeDtypeStruct((256, 256), BF16),
        jax.ShapeDtypeStruct((8, 256), F32),
        jax.ShapeDtypeStruct((256, 256), F32),
    )
    results = pl.pallas_call(
        functools.partial(kernel, tuple(buffers)),
        out_shape=shapes,
        in_specs=[anywhere] * 6,
        out_specs=(anywhere, anywhere, anywhere),
        scratch_shapes=list(buffers.values()),
        compiler_params=pltpu.CompilerParams(
            collective_id=0, has_side_effects=True, vmem_limit_bytes=60 * 1024 * 1024),
        name="graph_layer",
    )(tile_count, features, weight, tile_values, tile_coords.T, cotangent)
    return pl.pallas_call(
        hand_over, out_shape=shapes, in_specs=[anywhere] * 3, out_specs=(anywhere, anywhere, anywhere),
        scratch_shapes=[pltpu.VMEM(one.shape, one.dtype) for one in shapes] + [pltpu.SemaphoreType.DMA((6,))],
        name="hand_over",
    )(*results)


def solution(mesh):
    return jax.shard_map(
        per_device,
        mesh=mesh,
        in_specs=(
            P(("row", "col"), None),
            P(),
            P(("row", "col"), None, None),
            P(("row", "col"), None),
            P(("row", "col")),
            P(("row", "col"), None),
        ),
        out_specs=(P(("row", "col"), None), P("row", None), P(("row", "col"), None)),
        check_vma=False,
    )
```
